32 devices in a mesh: section: 2 (over core), dp: 16 (over z, y, x).
Axes of the slice: x: 2, y: 2, z: 4, core: 2. Of those that a mesh axis runs over, the one named last changes fastest.
Arguments:
- images: bfloat16 [64, 196, 512], P('dp'), may hold values from -6 to 6
- cotangent: bfloat16 [64, 196, 512], P('dp'), may hold values from -6 to 6
- image_count: int32 [16], P('dp'), may hold values from 1 to 4, as said below
- norm1_gain: float32 [2, 512], P('section'), may hold values from 0.5 to 1.5
- norm1_bias: float32 [2, 512], P('section'), may hold values from -3 to 3
- qkv_weight: bfloat16 [2, 512, 1536], P('section'), may hold values from -0.25 to 0.25
- query_bias: float32 [2, 512], P('section'), may hold values from -3 to 3
- value_bias: float32 [2, 512], P('section'), may hold values from -3 to 3
- bias_table: float32 [2, 169, 16], P('section'), may hold values from -4 to 4
- out_weight: bfloat16 [2, 512, 512], P('section'), may hold values from -0.75 to 0.75
- out_bias: float32 [2, 512], P('section'), may hold values from -3 to 3
- norm2_gain: float32 [2, 512], P('section'), may hold values from 0.5 to 1.5
- norm2_bias: float32 [2, 512], P('section'), may hold values from -3 to 3
- up_weight: bfloat16 [2, 512, 2048], P('section'), may hold values from -0.25 to 0.25
- up_bias: float32 [2, 2048], P('section'), may hold values from -3 to 3
- down_weight: bfloat16 [2, 2048, 512], P('section'), may hold values from -0.125 to 0.125
- down_bias: float32 [2, 512], P('section'), may hold values from -3 to 3
Outputs:
- segment_out: bfloat16 [2, 64, 196, 512], P('section', 'dp')
- input_grad: float32 [2, 64, 196, 512], P('section', 'dp')
- grad_norm1_gain: float32 [2, 512], P('section')
- grad_norm1_bias: float32 [2, 512], P('section')
- grad_qkv_weight: float32 [2, 512, 1536], P('section')
- grad_query_bias: float32 [2, 512], P('section')
- grad_value_bias: float32 [2, 512], P('section')
- grad_bias_table: float32 [2, 169, 16], P('section')
- grad_out_weight: float32 [2, 512, 512], P('section')
- grad_out_bias: float32 [2, 512], P('section')
- grad_norm2_gain: float32 [2, 512], P('section')
- grad_norm2_bias: float32 [2, 512], P('section')
- grad_up_weight: float32 [2, 512, 2048], P('section')
- grad_up_bias: float32 [2, 2048], P('section')
- grad_down_weight: float32 [2, 2048, 512], P('section')
- grad_down_bias: float32 [2, 512], P('section')
The draws below stay inside these ranges and needn't reach their ends.
Inputs may be any that keep to these rules, and one draw needn't show every extreme that they name: image_count of every dp index lies in 1 to 4; some index has all 4 slots live.
All inputs are finite; a program needn't handle non-finite values.
Results may differ from the reference program's by a relative error of at most 0.015.
Values may be sent and summed in bfloat16 or wider, within the bound.
No kernel may reach another device: no remote copies, remote signals or barrier semaphores. Data moves between devices by JAX's collectives and lax.ppermute only.
A program may use at most 192 MiB of HBM per device.

```python
import jax
import jax.numpy as jnp
from jax import lax

D = 512
HEADS = 16
FFN_DIM = 2048
WIN = 7
SIDE = 14
SHIFT = 3
IMG_DEV = 4
TOK = 196
TABLE = 169
IMAGES = 64


def draw_image_count(key, part):
    key_counts, key_full = jax.random.split(jax.random.fold_in(key, 17))
    devices_dp = IMAGES // IMG_DEV
    counts = jax.random.randint(key_counts, (devices_dp,), 1, IMG_DEV + 1)
    chosen = jax.random.randint(key_full, (), 0, devices_dp)
    return jnp.where(jnp.arange(devices_dp) == chosen, IMG_DEV, counts).astype(jnp.int32)


def shard_levels(own_key, extent, shards, least, top_value):
    def one(dim, blocks):
        steps = jax.random.uniform(jax.random.fold_in(jax.random.fold_in(own_key, 6), dim), (blocks,), jnp.float32, least / len(shards), top_value / len(shards))
        return jnp.repeat(jnp.exp(steps), extent[dim] // blocks).reshape((-1,) + (1,) * (len(extent) - dim - 1))

    loudness = one(*shards[0])
    for cut in shards[1:]:
        loudness = loudness * one(*cut)
    return loudness


def scatter_about(rng, extent, deviation, limit, cuts=(), held_as=jnp.bfloat16):
    values = deviation * jax.random.normal(rng, extent, jnp.float32)
    if cuts:
        values = values * shard_levels(rng, extent, cuts, -0.22, 0.18)
    return jnp.clip(values, -limit, limit).astype(held_as)


def setup_inputs(seed: int = 0) -> dict:
    key_list = jax.random.split(jax.random.key(seed), 18)
    images = scatter_about(key_list[0], (IMAGES, TOK, D), 1.0, 6.0, ((0, 16),))
    cotangent = scatter_about(key_list[1], (IMAGES, TOK, D), 1.0, 6.0, ((0, 16),))
    image_count = draw_image_count(jax.random.fold_in(key_list[17], 71), 0)
    norm1_gain = jnp.clip(1.0 + 0.1 * jax.random.normal(key_list[3], (2, D), jnp.float32), 0.5, 1.5)
    norm1_bias = scatter_about(key_list[4], (2, D), 0.5, 3.0, ((0, 2),), jnp.float32)
    qkv_weight = scatter_about(key_list[5], (2, D, 3 * D), D ** -0.5, 0.25, ((0, 2),))
    query_bias = scatter_about(key_list[6], (2, D), 0.5, 3.0, ((0, 2),), jnp.float32)
    value_bias = scatter_about(key_list[7], (2, D), 0.5, 3.0, ((0, 2),), jnp.float32)
    bias_table = scatter_about(key_list[8], (2, TABLE, HEADS), 1.0, 4.0, ((0, 2),), jnp.float32)
    out_weight = scatter_about(key_list[9], (2, D, D), (D // 7) ** -0.5, 0.75, ((0, 2),))
    out_bias = scatter_about(key_list[10], (2, D), 0.5, 3.0, ((0, 2),), jnp.float32)
    norm2_gain = jnp.clip(1.0 + 0.1 * jax.random.normal(key_list[11], (2, D), jnp.float32), 0.5, 1.5)
    norm2_bias = scatter_about(key_list[12], (2, D), 0.5, 3.0, ((0, 2),), jnp.float32)
    up_weight = scatter_about(key_list[13], (2, D, FFN_DIM), D ** -0.5, 0.25, ((0, 2),))
    up_bias = scatter_about(key_list[14], (2, FFN_DIM), 0.5, 3.0, ((0, 2),), jnp.float32)
    down_weight = scatter_about(key_list[15], (2, FFN_DIM, D), FFN_DIM ** -0.5, 0.125, ((0, 2),))
    down_bias = scatter_about(key_list[16], (2, D), 0.5, 3.0, ((0, 2),), jnp.float32)
    return {"images": images, "cotangent": cotangent, "image_count": image_count, "norm1_gain": norm1_gain, "norm1_bias": norm1_bias, "qkv_weight": qkv_weight, "query_bias": query_bias, "value_bias": value_bias, "bias_table": bias_table, "out_weight": out_weight, "out_bias": out_bias, "norm2_gain": norm2_gain, "norm2_bias": norm2_bias, "up_weight": up_weight, "up_bias": up_bias, "down_weight": down_weight, "down_bias": down_bias}


EPS = 1e-05
MASKED = -100.0
SQRT_HALF = 0.7071067811865476
INV_ROOT_TAU = 0.3989422804014327

def partition_grid(grid):
    count_img = grid.shape[0]
    chans = grid.shape[-1]
    across = SIDE // WIN
    grid = grid.reshape(count_img, across, WIN, across, WIN, chans).transpose(0, 1, 3, 2, 4, 5)
    return grid.reshape(count_img, across * across, WIN * WIN, chans)

def merge_grid(windows):
    count_img = windows.shape[0]
    chans = windows.shape[-1]
    across = SIDE // WIN
    grid = windows.reshape(count_img, across, across, WIN, WIN, chans).transpose(0, 1, 3, 2, 4, 5)
    return grid.reshape(count_img, SIDE, SIDE, chans)

def to_windows(token_rows, offset):
    grid = token_rows.reshape(token_rows.shape[0], SIDE, SIDE, token_rows.shape[-1])
    grid = jnp.roll(jnp.roll(grid, -offset, axis=1), -offset, axis=2)
    return partition_grid(grid)

def from_windows(windows, offset):
    grid = merge_grid(windows)
    grid = jnp.roll(jnp.roll(grid, offset, axis=1), offset, axis=2)
    return grid.reshape(grid.shape[0], SIDE * SIDE, grid.shape[-1])

def region_mask():
    places = jnp.arange(SIDE)
    labels = (places >= SIDE - WIN).astype(jnp.int32) + (places >= SIDE - SHIFT).astype(jnp.int32)
    region = labels[:, None] * 3 + labels[None, :]
    windows = partition_grid(region[None, :, :, None])[0, :, :, 0]
    return jnp.where(windows[:, :, None] != windows[:, None, :], MASKED, 0.0).astype(jnp.float32)

def position_onehot():
    cells = jnp.arange(WIN * WIN)
    row_of = cells // WIN
    col_of = cells % WIN
    index = (row_of[:, None] - row_of[None, :] + WIN - 1) * (2 * WIN - 1) + col_of[:, None] - col_of[None, :] + WIN - 1
    entries = jnp.arange((2 * WIN - 1) * (2 * WIN - 1))
    return (index.reshape(-1)[:, None] == entries[None, :]).astype(jnp.float32)

def relative_bias(table):
    spread_bias = jnp.dot(position_onehot(), table.astype(jnp.float32), precision=lax.Precision.HIGHEST)
    return spread_bias.reshape(WIN * WIN, WIN * WIN, -1).transpose(2, 0, 1)

def normalize(values):
    centered = values - lax.optimization_barrier(jnp.mean(values, axis=-1, keepdims=True))
    inv_std = lax.rsqrt(lax.optimization_barrier(jnp.mean(centered * centered, axis=-1, keepdims=True)) + EPS)
    return (centered * inv_std, inv_std)

def norm_back(upstream, scaled, inv_std, gain):
    along = upstream * gain
    return inv_std * (along - lax.optimization_barrier(jnp.mean(along, axis=-1, keepdims=True)) - scaled * lax.optimization_barrier(jnp.mean(along * scaled, axis=-1, keepdims=True)))

def gelu_parts(hidden_pre):
    cdf_val = 0.5 * (1.0 + lax.erf(hidden_pre * SQRT_HALF))
    density = jnp.exp(-0.5 * hidden_pre * hidden_pre) * INV_ROOT_TAU
    return (hidden_pre * cdf_val, cdf_val + hidden_pre * density)

def batched(form, left, right):
    return jnp.einsum(form, left.astype(jnp.float32), right.astype(jnp.float32))

def layer_pieces(layer_in, params, offset, mask_on):
    gain_one, bias_one, w_qkv, q_bias, v_bias, table, w_out, o_bias, gain_two, bias_two, w_up, up_shift, w_down, down_shift = params
    width = w_out.shape[0]
    heads = table.shape[1]
    head_dim = width // heads
    flat_in = layer_in.astype(jnp.float32)
    scaled_one, inv_one = normalize(flat_in)
    normed = (scaled_one * gain_one + bias_one).astype(jnp.bfloat16)
    win_rows = to_windows(normed, offset)
    shape_w = win_rows.shape
    qkv = jnp.dot(win_rows.reshape(-1, width), w_qkv, preferred_element_type=jnp.float32)
    factor = head_dim ** (-0.5)
    head_shape = shape_w[:3] + (heads, head_dim)
    query = ((qkv[:, :width] + q_bias) * factor).astype(jnp.bfloat16).reshape(head_shape)
    keys = qkv[:, width:2 * width].astype(jnp.bfloat16).reshape(head_shape)
    values_v = (qkv[:, 2 * width:] + v_bias).astype(jnp.bfloat16).reshape(head_shape)
    scores = batched('bwihe,bwjhe->bwhij', query, keys) + relative_bias(table)[None, None]
    scores = scores + (mask_on * region_mask())[None, :, None]
    peak = lax.optimization_barrier(jnp.max(scores, axis=-1, keepdims=True))
    expo = jnp.exp(scores - peak)
    prob = expo / lax.optimization_barrier(jnp.sum(expo, axis=-1, keepdims=True))
    prob_b = prob.astype(jnp.bfloat16)
    mixed = batched('bwhij,bwjhe->bwihe', prob_b, values_v).astype(jnp.bfloat16).reshape(shape_w)
    attn_flat = from_windows(mixed, offset).reshape(-1, width)
    resid = flat_in + (jnp.dot(attn_flat, w_out, preferred_element_type=jnp.float32) + o_bias).reshape(flat_in.shape)
    scaled_two, inv_two = normalize(resid)
    normed_two = (scaled_two * gain_two + bias_two).astype(jnp.bfloat16).reshape(-1, width)
    hidden_pre = jnp.dot(normed_two, w_up, preferred_element_type=jnp.float32) + up_shift
    activ, slope = gelu_parts(hidden_pre)
    activ_b = activ.astype(jnp.bfloat16)
    output = resid + (jnp.dot(activ_b, w_down, preferred_element_type=jnp.float32) + down_shift).reshape(flat_in.shape)
    return dict(output=output, scaled_one=scaled_one, inv_one=inv_one, win_rows=win_rows, query=query, keys=keys, values_v=values_v, prob=prob, prob_b=prob_b, attn_flat=attn_flat, scaled_two=scaled_two, inv_two=inv_two, normed_two=normed_two, slope=slope, activ_b=activ_b)

def layer_forward(layer_in, params, offset, mask_on):
    return layer_pieces(layer_in, params, offset, mask_on)['output'].astype(jnp.bfloat16)

def layer_backward(layer_in, upstream, params, offset, mask_on):
    gain_one, bias_one, w_qkv, q_bias, v_bias, table, w_out, o_bias, gain_two, bias_two, w_up, up_shift, w_down, down_shift = params
    kept = layer_pieces(layer_in, params, offset, mask_on)
    width = w_out.shape[0]
    heads = table.shape[1]
    head_dim = width // heads
    factor = head_dim ** (-0.5)
    shape_w = kept['win_rows'].shape
    head_shape = shape_w[:3] + (heads, head_dim)
    up_flat = upstream.reshape(-1, width)
    up_b16 = up_flat.astype(jnp.bfloat16)
    g_down = jnp.dot(kept['activ_b'].T, up_b16, preferred_element_type=jnp.float32)
    g_down_b = lax.optimization_barrier(jnp.sum(up_flat, axis=0))
    d_pre = jnp.dot(up_b16, w_down.T, preferred_element_type=jnp.float32) * kept['slope']
    d_pre_b = d_pre.astype(jnp.bfloat16)
    g_up = jnp.dot(kept['normed_two'].T, d_pre_b, preferred_element_type=jnp.float32)
    g_up_b = lax.optimization_barrier(jnp.sum(d_pre, axis=0))
    d_n2 = jnp.dot(d_pre_b, w_up.T, preferred_element_type=jnp.float32).reshape(upstream.shape)
    g_gain_two = lax.optimization_barrier(jnp.sum(d_n2 * kept['scaled_two'], axis=(0, 1)))
    g_bias_two = lax.optimization_barrier(jnp.sum(d_n2, axis=(0, 1)))
    d_resid = upstream + norm_back(d_n2, kept['scaled_two'], kept['inv_two'], gain_two)
    d_resid_flat = d_resid.reshape(-1, width)
    d_resid_b = d_resid_flat.astype(jnp.bfloat16)
    g_out = jnp.dot(kept['attn_flat'].T, d_resid_b, preferred_element_type=jnp.float32)
    g_out_b = lax.optimization_barrier(jnp.sum(d_resid_flat, axis=0))
    d_mixed = jnp.dot(d_resid_b, w_out.T, preferred_element_type=jnp.float32).astype(jnp.bfloat16)
    d_mixed_w = to_windows(d_mixed.reshape(upstream.shape), offset).reshape(head_shape)
    d_prob = batched('bwihe,bwjhe->bwhij', d_mixed_w, kept['values_v'])
    d_values = batched('bwhij,bwihe->bwjhe', kept['prob_b'], d_mixed_w)
    prob = kept['prob']
    d_scores = prob * (d_prob - lax.optimization_barrier(jnp.sum(prob * d_prob, axis=-1, keepdims=True)))
    summed = lax.optimization_barrier(jnp.sum(d_scores, axis=(0, 1))).transpose(1, 2, 0).reshape(WIN * WIN * WIN * WIN, heads)
    g_table = jnp.dot(position_onehot().T, summed, precision=lax.Precision.HIGHEST)
    d_scores_b = d_scores.astype(jnp.bfloat16)
    d_query = batched('bwhij,bwjhe->bwihe', d_scores_b, kept['keys']).reshape(-1, width) * factor
    d_keys = batched('bwhij,bwihe->bwjhe', d_scores_b, kept['query']).reshape(-1, width)
    d_values = d_values.reshape(-1, width)
    g_q_bias = lax.optimization_barrier(jnp.sum(d_query, axis=0))
    g_v_bias = lax.optimization_barrier(jnp.sum(d_values, axis=0))
    d_qkv_b = jnp.concatenate([d_query, d_keys, d_values], axis=1).astype(jnp.bfloat16)
    g_qkv = jnp.dot(kept['win_rows'].reshape(-1, width).T, d_qkv_b, preferred_element_type=jnp.float32)
    d_normed = jnp.dot(d_qkv_b, w_qkv.T, preferred_element_type=jnp.float32).reshape(shape_w)
    d_normed_rows = from_windows(d_normed, offset)
    g_gain_one = lax.optimization_barrier(jnp.sum(d_normed_rows * kept['scaled_one'], axis=(0, 1)))
    g_bias_one = lax.optimization_barrier(jnp.sum(d_normed_rows, axis=(0, 1)))
    d_input = d_resid + norm_back(d_normed_rows, kept['scaled_one'], kept['inv_one'], gain_one)
    return (d_input, (g_gain_one, g_bias_one, g_qkv, g_q_bias, g_v_bias, g_table, g_out, g_out_b, g_gain_two, g_bias_two, g_up, g_up_b, g_down, g_down_b))

def reference(images, cotangent, image_count, norm1_gain, norm1_bias, qkv_weight, query_bias, value_bias, bias_table, out_weight, out_bias, norm2_gain, norm2_bias, up_weight, up_bias, down_weight, down_bias):
    params = (norm1_gain, norm1_bias, qkv_weight, query_bias, value_bias, bias_table, out_weight, out_bias, norm2_gain, norm2_bias, up_weight, up_bias, down_weight, down_bias)
    first = tuple((weight[0] for weight in params))
    second = tuple((weight[1] for weight in params))
    devices_dp = images.shape[0] // IMG_DEV
    slots = jnp.arange(IMG_DEV)
    width = images.shape[-1]
    image_blocks = images.reshape(devices_dp, IMG_DEV, SIDE * SIDE, width)
    cot_blocks = cotangent.reshape(devices_dp, IMG_DEV, SIDE * SIDE, width)

    def step_block(totals, inputs):
        block_img, block_cot, block_count = inputs
        live = (slots < block_count).astype(jnp.float32)[:, None, None]
        out_zero = layer_forward(block_img, first, 0, 0.0)
        out_one = layer_forward(out_zero, second, SHIFT, 1.0)
        grad_up = block_cot.astype(jnp.float32) * live
        in_grad_one, grads_one = layer_backward(out_zero, grad_up, second, SHIFT, 1.0)
        sent_back = lax.optimization_barrier(in_grad_one.astype(jnp.bfloat16)).astype(jnp.float32)
        in_grad_zero, grads_zero = layer_backward(block_img, sent_back, first, 0, 0.0)
        totals = tuple((total + jnp.stack([part_a, part_b]) for total, part_a, part_b in zip(totals, grads_zero, grads_one)))
        return (totals, (jnp.stack([out_zero, out_one]), jnp.stack([in_grad_zero, in_grad_one])))
    start = tuple((jnp.zeros(weight.shape, jnp.float32) for weight in params))
    totals, (outs, in_grads) = lax.scan(step_block, start, (image_blocks, cot_blocks, image_count))
    segment_out = outs.transpose(1, 0, 2, 3, 4).reshape(2, devices_dp * IMG_DEV, SIDE * SIDE, width)
    input_grad = in_grads.transpose(1, 0, 2, 3, 4).reshape(2, devices_dp * IMG_DEV, SIDE * SIDE, width)
    return (segment_out, input_grad, totals[0], totals[1], totals[2], totals[3], totals[4], totals[5], totals[6], totals[7], totals[8], totals[9], totals[10], totals[11], totals[12], totals[13])
```

```python
import functools

import jax
import jax.numpy as jnp
import numpy as np
from jax import lax
from jax.experimental import pallas as pl
from jax.experimental.pallas import tpu as pltpu
from jax.sharding import PartitionSpec as P

WIN = 7
SIDE = 14
SHIFT = 3
CELLS = WIN * WIN
PADW = 64
NWIN = (SIDE // WIN) ** 2
IROWS = NWIN * PADW
GROUP = 4
LANES = 128
FCHUNK = 512
EPS = 1e-05
MASKED = -100.0
PADDED = -1e30
SQRT_HALF = 0.7071067811865476
INV_ROOT_TAU = 0.3989422804014327
F32 = jnp.float32
BF16 = jnp.bfloat16
SMALL_ROWS = 16


def window_source(offset):
    across = SIDE // WIN
    places = np.arange(SIDE * SIDE)
    window_no = places // CELLS
    cell_no = places % CELLS
    grid_row = window_no // across * WIN + cell_no // WIN
    grid_col = window_no % across * WIN + cell_no % WIN
    source = (grid_row + offset) % SIDE * SIDE + (grid_col + offset) % SIDE
    return window_no * PADW + cell_no, source


def window_onehot(offset):
    rows, source = window_source(offset)
    table = np.zeros((IROWS, SIDE * SIDE), np.float32)
    table[rows, source] = 1.0
    return table


def region_mask():
    places = np.arange(SIDE)
    labels = (places >= SIDE - WIN).astype(np.int32) + (places >= SIDE - SHIFT).astype(np.int32)
    region = (labels[:, None] * 3 + labels[None, :]).reshape(-1)
    rows, source = window_source(0)
    padded = np.full((IROWS,), -1)
    padded[rows] = region[source]
    padded = padded.reshape(NWIN, PADW)
    differ = (padded[:, :, None] != padded[:, None, :]) & (padded[:, :, None] >= 0)
    differ &= padded[:, None, :] >= 0
    return np.where(differ, MASKED, 0.0).astype(np.float32)


def relative_index():
    cells = np.arange(CELLS)
    row_of, col_of = cells // WIN, cells % WIN
    row_gap = row_of[:, None] - row_of[None, :] + WIN - 1
    return row_gap * (2 * WIN - 1) + col_of[:, None] - col_of[None, :] + WIN - 1


def pair_onehot():
    index = np.full((PADW, PADW), -1, np.int32)
    index[:CELLS, :CELLS] = relative_index().T
    entries = jnp.arange((2 * WIN - 1) ** 2)
    return (jnp.asarray(index)[:, :, None] == entries).astype(F32)


def bias_tiles(table, mask_on):
    heads = table.shape[1]
    spread = jnp.einsum("jit,th->hji", pair_onehot(), table, precision=lax.Precision.HIGHEST)
    tiles = spread.reshape(heads // GROUP, GROUP, PADW, PADW).transpose(0, 2, 1, 3)
    pad_key = np.where(np.arange(PADW) >= CELLS, PADDED, 0.0).astype(np.float32)
    tiles = tiles + pad_key[None, :, None, None]
    if mask_on:
        tiles = tiles[None] + region_mask()[:, None, :, None, :]
    else:
        tiles = tiles[None]
    return tiles.reshape(tiles.shape[0], heads // GROUP, PADW, GROUP * PADW)


def table_grad(tiles, heads):
    spread = tiles.reshape(heads // GROUP, PADW, GROUP, PADW).transpose(0, 2, 1, 3)
    spread = spread.reshape(heads, PADW, PADW)
    return jnp.einsum("jit,hji->th", pair_onehot(), spread, precision=lax.Precision.HIGHEST)


def dot_nn(left, right):
    return lax.dot_general(left, right, (((1,), (0,)), ((), ())), preferred_element_type=F32)


def dot_nt(left, right):
    return lax.dot_general(left, right, (((1,), (1,)), ((), ())), preferred_element_type=F32)


def dot_tn(left, right):
    return lax.dot_general(left, right, (((0,), (0,)), ((), ())), preferred_element_type=F32)


def normalize(values):
    centered = values - jnp.mean(values, axis=-1, keepdims=True)
    inv_std = lax.rsqrt(jnp.mean(centered * centered, axis=-1, keepdims=True) + EPS)
    return centered * inv_std, inv_std


def norm_back(upstream, scaled, inv_std, gain):
    along = upstream * gain
    return inv_std * (
        along
        - jnp.mean(along, axis=-1, keepdims=True)
        - scaled * jnp.mean(along * scaled, axis=-1, keepdims=True)
    )


def gelu_parts(pre):
    cdf_val = 0.5 * (1.0 + lax.erf(pre * SQRT_HALF))
    density = jnp.exp(-0.5 * pre * pre) * INV_ROOT_TAU
    return pre * cdf_val, cdf_val + pre * density


def head_mask(head_dim):
    rows = lax.broadcasted_iota(jnp.int32, (GROUP * PADW, LANES), 0) // PADW
    cols = lax.broadcasted_iota(jnp.int32, (GROUP * PADW, LANES), 1) // head_dim
    return jnp.where(rows == cols, 1.0, 0.0).astype(BF16)


def expand(tile, mask):
    return jnp.concatenate([tile] * GROUP, axis=0) * mask


def collapse(wide, head_dim):
    head_of = lax.broadcasted_iota(jnp.int32, (PADW, LANES), 1) // head_dim
    total = wide[:PADW]
    for head in range(1, GROUP):
        total = jnp.where(head_of == head, wide[head * PADW : (head + 1) * PADW], total)
    return total


def rows_at(number, size):
    return pl.ds(pl.multiple_of(number * size, size), size)


def forward_kernel(
    base_ref, x_ref, perm_ref, bias_ref, vec_ref, wqkv_ref, wout_ref, wup_ref, wdown_ref,
    out_ref, xa_ref, nrm_ref, qkv_ref, prob_ref, mix_ref, res_ref, n2_ref, act_ref, slope_ref,
    *, images, head_dim, masked,
):
    width = wout_ref.shape[0]
    hidden = wup_ref.shape[1]
    groups = width // LANES
    factor = head_dim ** (-0.5)
    first = base_ref[0]

    def enter(img, carry):
        rows = rows_at(img, IROWS)
        entry = dot_nn(perm_ref[...], x_ref[first + img])
        xa_ref[rows, :] = entry.astype(BF16)
        scaled, _ = normalize(entry)
        normed = (scaled * vec_ref[0:1, :] + vec_ref[1:2, :]).astype(BF16)
        nrm_ref[rows, :] = normed
        query = (dot_nn(normed, wqkv_ref[:, :width]) + vec_ref[2:3, :]) * factor
        qkv_ref[rows, :width] = query.astype(BF16)
        qkv_ref[rows, width : 2 * width] = dot_nn(normed, wqkv_ref[:, width : 2 * width]).astype(BF16)
        value = dot_nn(normed, wqkv_ref[:, 2 * width :]) + vec_ref[3:4, :]
        qkv_ref[rows, 2 * width :] = value.astype(BF16)
        return carry

    lax.fori_loop(0, images, enter, 0)
    mask = head_mask(head_dim)

    def attend(win, carry):
        rows = rows_at(win, PADW)
        bias_no = win % NWIN if masked else 0
        for grp in range(groups):
            at = grp * LANES
            query = qkv_ref[rows, at : at + LANES]
            key = qkv_ref[rows, width + at : width + at + LANES]
            value = qkv_ref[rows, 2 * width + at : 2 * width + at + LANES]
            score = dot_nt(key, expand(query, mask)) + bias_ref[bias_no, grp]
            expo = jnp.exp(score - jnp.max(score, axis=0, keepdims=True))
            prob = expo * (1.0 / jnp.sum(expo, axis=0, keepdims=True))
            prob_ref[win, grp] = prob
            wide = dot_tn(prob.astype(BF16), value)
            mix_ref[rows, at : at + LANES] = collapse(wide, head_dim).astype(BF16)
        return carry

    lax.fori_loop(0, images * NWIN, attend, 0)

    def leave(img, carry):
        rows = rows_at(img, IROWS)
        entry = xa_ref[rows, :].astype(F32)
        resid = entry + dot_nn(mix_ref[rows, :], wout_ref[...]) + vec_ref[4:5, :]
        res_ref[rows, :] = resid
        scaled, _ = normalize(resid)
        n2_ref[rows, :] = (scaled * vec_ref[5:6, :] + vec_ref[6:7, :]).astype(BF16)
        for part in range(hidden // FCHUNK):
            at = part * FCHUNK
            pre = dot_nn(n2_ref[rows, :], wup_ref[:, at : at + FCHUNK]) + vec_ref[8 + part : 9 + part, :]
            activ, slope = gelu_parts(pre)
            act_ref[rows, at : at + FCHUNK] = activ.astype(BF16)
            slope_ref[rows, at : at + FCHUNK] = slope
        done = res_ref[rows, :] + dot_nn(act_ref[rows, :], wdown_ref[...]) + vec_ref[7:8, :]
        out_ref[img] = dot_tn(perm_ref[...], done.astype(BF16)).astype(BF16)
        return carry

    lax.fori_loop(0, images, leave, 0)


def ffn_back_kernel(
    base_ref, g_ref, live_ref, perm_ref, vec_ref, wout_ref, wup_ref, wdown_ref,
    mix_ref, res_ref, n2_ref, act_ref, slope_ref,
    dres_ref, dmix_ref, keep_down_ref, send_down_ref, keep_up_ref, send_up_ref, keep_out_ref, send_out_ref,
    small_ref, gb_ref, dpre_ref, dresb_ref,
    *, images,
):
    width = wout_ref.shape[0]
    hidden = wup_ref.shape[1]
    first = base_ref[0]
    section = base_ref[1]
    small_ref[...] = jnp.zeros_like(small_ref)

    def step(img, carry):
        rows = rows_at(img, IROWS)
        upstream = dot_nn(perm_ref[...], g_ref[first + img]) * live_ref[img]
        gb_ref[rows, :] = upstream.astype(BF16)
        small_ref[7:8, :] += jnp.sum(upstream, axis=0, keepdims=True)
        for part in range(hidden // FCHUNK):
            at = part * FCHUNK
            dpre = dot_nt(gb_ref[rows, :], wdown_ref[at : at + FCHUNK, :]) * slope_ref[rows, at : at + FCHUNK]
            small_ref[8 + part : 9 + part, :] += jnp.sum(dpre, axis=0, keepdims=True)
            dpre_ref[rows, at : at + FCHUNK] = dpre.astype(BF16)
        dnorm = dot_nt(dpre_ref[rows, :], wup_ref[...])
        scaled, inv_std = normalize(res_ref[rows, :])
        small_ref[5:6, :] += jnp.sum(dnorm * scaled, axis=0, keepdims=True)
        small_ref[6:7, :] += jnp.sum(dnorm, axis=0, keepdims=True)
        dres = gb_ref[rows, :].astype(F32) + norm_back(dnorm, scaled, inv_std, vec_ref[5:6, :])
        dres_ref[rows, :] = dres
        small_ref[4:5, :] += jnp.sum(dres, axis=0, keepdims=True)
        dresb_ref[rows, :] = dres.astype(BF16)
        dmix_ref[rows, :] = dot_nt(dresb_ref[rows, :], wout_ref[...]).astype(BF16)
        return carry

    lax.fori_loop(0, images, step, 0)
    for side, down, up, out in ((0, keep_down_ref, keep_up_ref, keep_out_ref), (1, send_down_ref, send_up_ref, send_out_ref)):
        half = section if side == 0 else 1 - section
        span = hidden // 2
        for part in range(span // FCHUNK):
            cols = pl.ds(pl.multiple_of(half * span + part * FCHUNK, FCHUNK), FCHUNK)
            down[part * FCHUNK : (part + 1) * FCHUNK, :] = dot_tn(act_ref[:, cols], gb_ref[...]).astype(BF16)
        cols = rows_at(half, width // 2)
        for part in range(hidden // width):
            at = part * width
            block = dot_tn(n2_ref[:, cols], dpre_ref[:, at : at + width])
            up[part * (width // 2) : (part + 1) * (width // 2), :] = block.astype(BF16)
        out[...] = dot_tn(mix_ref[:, cols], dresb_ref[...]).astype(BF16)


def attn_back_kernel(
    base_ref, perm_ref, vec_ref, wqkv_ref, xa_ref, nrm_ref, qkv_ref, prob_ref, dres_ref, dmix_ref,
    igrad_ref, igrad_b_ref, keep_ref, send_ref, tiles_ref, small_ref, dqkv_ref,
    *, images, head_dim,
):
    width = wqkv_ref.shape[0]
    groups = width // LANES
    factor = head_dim ** (-0.5)
    section = base_ref[1]
    small_ref[...] = jnp.zeros_like(small_ref)
    tiles_ref[...] = jnp.zeros_like(tiles_ref)
    mask = head_mask(head_dim)

    def attend(win, carry):
        rows = rows_at(win, PADW)
        for grp in range(groups):
            at = grp * LANES
            query = qkv_ref[rows, at : at + LANES]
            key = qkv_ref[rows, width + at : width + at + LANES]
            value = qkv_ref[rows, 2 * width + at : 2 * width + at + LANES]
            dmix = expand(dmix_ref[rows, at : at + LANES], mask)
            prob = prob_ref[win, grp]
            dprob = dot_nt(value, dmix)
            dvalue = dot_nn(prob.astype(BF16), dmix)
            dscore = prob * (dprob - jnp.sum(prob * dprob, axis=0, keepdims=True))
            tiles_ref[grp] += dscore
            dscore_b = dscore.astype(BF16)
            dkey = dot_nn(dscore_b, expand(query, mask))
            dquery = collapse(dot_tn(dscore_b, key), head_dim) * factor
            small_ref[2:3, at : at + LANES] += jnp.sum(dquery, axis=0, keepdims=True)
            small_ref[3:4, at : at + LANES] += jnp.sum(dvalue, axis=0, keepdims=True)
            dqkv_ref[rows, at : at + LANES] = dquery.astype(BF16)
            dqkv_ref[rows, width + at : width + at + LANES] = dkey.astype(BF16)
            dqkv_ref[rows, 2 * width + at : 2 * width + at + LANES] = dvalue.astype(BF16)
        return carry

    lax.fori_loop(0, images * NWIN, attend, 0)

    def leave(img, carry):
        rows = rows_at(img, IROWS)
        dnorm = dot_nt(dqkv_ref[rows, :], wqkv_ref[...])
        scaled, inv_std = normalize(xa_ref[rows, :].astype(F32))
        small_ref[0:1, :] += jnp.sum(dnorm * scaled, axis=0, keepdims=True)
        small_ref[1:2, :] += jnp.sum(dnorm, axis=0, keepdims=True)
        grad = dres_ref[rows, :] + norm_back(dnorm, scaled, inv_std, vec_ref[0:1, :])
        high = grad.astype(BF16)
        low = (grad - high.astype(F32)).astype(BF16)
        moved = dot_tn(perm_ref[...], high)
        igrad_b_ref[img] = moved.astype(BF16)
        igrad_ref[img] = moved + dot_tn(perm_ref[...], low)
        return carry

    lax.fori_loop(0, images, leave, 0)
    for side, dest in ((0, keep_ref), (1, send_ref)):
        half = section if side == 0 else 1 - section
        cols = rows_at(half, width // 2)
        for part in range(3):
            at = part * width
            block = dot_tn(nrm_ref[:, cols], dqkv_ref[:, at : at + width])
            dest[part * (width // 2) : (part + 1) * (width // 2), :] = block.astype(BF16)


def vmem():
    return pl.BlockSpec(memory_space=pltpu.VMEM)


def smem():
    return pl.BlockSpec(memory_space=pltpu.SMEM)


def shape_of(shape, dtype):
    return jax.ShapeDtypeStruct(shape, dtype)


PARAMS = pltpu.CompilerParams(vmem_limit_bytes=60 * 1024 * 1024)


def run_forward(base, rows_in, perm, bias, vec, weights, images, head_dim, masked):
    wqkv, wout, wup, wdown = weights
    width, hidden = wup.shape
    total = images * IROWS
    shapes = (
        shape_of((images, SIDE * SIDE, width), BF16),
        shape_of((total, width), BF16),
        shape_of((total, width), BF16),
        shape_of((total, 3 * width), BF16),
        shape_of((images * NWIN, width // LANES, PADW, GROUP * PADW), F32),
        shape_of((total, width), BF16),
        shape_of((total, width), F32),
        shape_of((total, width), BF16),
        shape_of((total, hidden), BF16),
        shape_of((total, hidden), F32),
    )
    return pl.pallas_call(
        functools.partial(forward_kernel, images=images, head_dim=head_dim, masked=masked),
        out_shape=shapes,
        in_specs=[smem()] + [vmem()] * 8,
        out_specs=tuple(vmem() for _ in shapes),
        compiler_params=PARAMS,
        name="layer_forward",
    )(base, rows_in, perm, bias, vec, wqkv, wout, wup, wdown)


def run_ffn_back(base, g_rows, live, perm, vec, weights, kept, images):
    _, wout, wup, wdown = weights
    _, _, _, _, mix, res, n2, act, slope = kept
    width, hidden = wup.shape
    total = images * IROWS
    shapes = (
        shape_of((total, width), F32),
        shape_of((total, width), BF16),
        shape_of((hidden // 2, width), BF16),
        shape_of((hidden // 2, width), BF16),
        shape_of((hidden // 2, width), BF16),
        shape_of((hidden // 2, width), BF16),
        shape_of((width // 2, width), BF16),
        shape_of((width // 2, width), BF16),
        shape_of((SMALL_ROWS, width), F32),
    )
    return pl.pallas_call(
        functools.partial(ffn_back_kernel, images=images),
        out_shape=shapes,
        in_specs=[smem(), vmem(), smem()] + [vmem()] * 10,
        out_specs=tuple(vmem() for _ in shapes),
        scratch_shapes=[
            pltpu.VMEM((total, width), BF16),
            pltpu.VMEM((total, hidden), BF16),
            pltpu.VMEM((total, width), BF16),
        ],
        compiler_params=PARAMS,
        name="ffn_back",
    )(base, g_rows, live, perm, vec, wout, wup, wdown, mix, res, n2, act, slope)


def run_attn_back(base, perm, vec, weights, kept, dres, dmix, images, head_dim):
    wqkv = weights[0]
    xa, nrm, qkv, prob = kept[:4]
    width = wqkv.shape[0]
    total = images * IROWS
    shapes = (
        shape_of((images, SIDE * SIDE, width), F32),
        shape_of((images, SIDE * SIDE, width), BF16),
        shape_of((3 * width // 2, width), BF16),
        shape_of((3 * width // 2, width), BF16),
        shape_of((width // LANES, PADW, GROUP * PADW), F32),
        shape_of((SMALL_ROWS, width), F32),
    )
    return pl.pallas_call(
        functools.partial(attn_back_kernel, images=images, head_dim=head_dim),
        out_shape=shapes,
        in_specs=[smem()] + [vmem()] * 9,
        out_specs=tuple(vmem() for _ in shapes),
        scratch_shapes=[pltpu.VMEM((total, 3 * width), BF16)],
        compiler_params=PARAMS,
        name="attn_back",
    )(base, perm, vec, wqkv, xa, nrm, qkv, prob, dres, dmix)


def round_orders(bits):
    if bits == 4:
        return ((0, 1, 2, 3), (1, 0, 3, 2), (2, 3, 0, 1), (3, 2, 0, 1))
    axes = list(range(bits))
    return tuple(tuple(axes[turn:] + axes[:turn]) for turn in range(4))


def first_sum_kernel(bit_ref, *refs):
    keep, recv, outs, total_ref = refs[:4], refs[4:8], refs[8:16], refs[16]
    at = 0
    for mine, other in zip(keep, recv):
        size = mine.shape[0]
        total_ref[at : at + size, :] = (mine[...].astype(F32) + other[...].astype(F32)).astype(BF16)
        at += size
    at = 0
    for color in range(4):
        half = outs[color].shape[0]
        bit = bit_ref[color]
        outs[color][...] = total_ref[pl.ds(pl.multiple_of(at + bit * half, 8), half), :]
        outs[4 + color][...] = total_ref[pl.ds(pl.multiple_of(at + (1 - bit) * half, 8), half), :]
        at += 2 * half


def sum_kernel(bit_ref, *refs):
    keep, recv, outs = refs[:4], refs[4:8], refs[8:]
    for color in range(4):
        size = keep[color].shape[0]
        if len(outs) == 4:
            outs[color][...] = (keep[color][...].astype(F32) + recv[color][...].astype(F32)).astype(BF16)
            continue
        half = size // 2
        bit = bit_ref[color]
        for side, start in ((0, bit * half), (4, (1 - bit) * half)):
            rows = pl.ds(pl.multiple_of(start, 8), half)
            summed = keep[color][rows, :].astype(F32) + recv[color][rows, :].astype(F32)
            outs[side + color][...] = summed.astype(BF16)


def merge_kernel(bit_ref, *refs):
    own, recv, outs = refs[:4], refs[4:8], refs[8:]
    for color in range(4):
        size = own[color].shape[1]
        bit = bit_ref[color]
        outs[color][:, pl.ds(pl.multiple_of(bit * size, 8), size), :] = own[color][...]
        outs[color][:, pl.ds(pl.multiple_of((1 - bit) * size, 8), size), :] = recv[color][...]


def final_kernel(bit_ref, *refs):
    own, recv = refs[:4], refs[4:8]
    down_ref, up_ref, out_ref, qkv_ref = refs[8:]
    width = out_ref.shape[1]
    part = width // 2
    for half in range(2):
        rows = slice(half * part, (half + 1) * part)
        bit = bit_ref[0]
        span = own[0].shape[1]
        for side, source in ((bit, own[0]), (1 - bit, recv[0])):
            down_ref[pl.ds(pl.multiple_of(half * 2 * span + side * span, span), span), :] = source[half].astype(F32)
        bit = bit_ref[1]
        blocks = own[1].shape[1] // part
        for side, source in ((bit, own[1]), (1 - bit, recv[1])):
            for block in range(blocks):
                cols = pl.ds(pl.multiple_of((side * blocks + block) * width, width), width)
                up_ref[rows, cols] = source[half, block * part : (block + 1) * part, :].astype(F32)
        is_low = bit_ref[2] == 0
        mine, other = own[2][half].astype(F32), recv[2][half].astype(F32)
        out_ref[rows, :] = jnp.where(is_low, mine, other)
        qkv_ref[rows, :width] = jnp.where(is_low, other, mine)
        bit = bit_ref[3]
        for side, source in ((bit, own[3]), (1 - bit, recv[3])):
            cols = pl.ds(pl.multiple_of((1 + side) * width, width), width)
            qkv_ref[rows, cols] = source[half].astype(F32)


def small_call(kernel, name, bits, arrays, shapes, scratch=()):
    return pl.pallas_call(
        kernel,
        out_shape=tuple(shapes),
        in_specs=[smem()] + [vmem()] * len(arrays),
        out_specs=tuple(vmem() for _ in shapes),
        scratch_shapes=list(scratch),
        compiler_params=PARAMS,
        name=name,
    )(bits, *arrays)


def exchange(value, bit, count):
    return lax.ppermute(value, "dp", [(one, one ^ (1 << bit)) for one in range(count)])


def reduce_shards(keep, send, orders, place_bits, count):
    recv = [swap(part) for part in send]
    width = keep[0].shape[1]
    total = sum(part.shape[0] for part in keep)
    sizes = [total // 3, total // 3, total // 6, total // 6]
    halves = [shape_of((size // 2, width), BF16) for size in sizes]
    parts = small_call(first_sum_kernel, "sum_first", place_bits[0], list(keep) + recv, halves * 2,
                       [pltpu.VMEM((total, width), BF16)])
    rounds = len(orders[0])
    for turn in range(rounds):
        mine, gone = parts[:4], parts[4:]
        recv = [exchange(part, order[turn], count) for part, order in zip(gone, orders)]
        if turn + 1 < rounds:
            halves = [shape_of((part.shape[0] // 2, width), BF16) for part in mine]
            parts = small_call(sum_kernel, "sum_round", place_bits[turn + 1], list(mine) + recv, halves * 2)
        else:
            halves = [shape_of(part.shape, BF16) for part in mine]
            parts = small_call(sum_kernel, "sum_last", place_bits[turn], list(mine) + recv, halves)
    return parts


def gather_layer(shards_zero, shards_one, section, orders, place_bits, count):
    parts = []
    for zero, one in zip(shards_zero, shards_one):
        own = jnp.where(section == 0, zero, one)
        got = swap(jnp.where(section == 0, one, zero))
        parts.append(jnp.where(section == 0, jnp.stack([own, got]), jnp.stack([got, own])))
    rounds = len(orders[0])
    width = parts[0].shape[-1]
    for turn in reversed(range(rounds)):
        recv = [exchange(part, order[turn], count) for part, order in zip(parts, orders)]
        if turn:
            shapes = [shape_of((2, 2 * part.shape[1], width), BF16) for part in parts]
            parts = small_call(merge_kernel, "merge_round", place_bits[turn], list(parts) + recv, shapes)
    hidden = 4 * parts[0].shape[1]
    shapes = [shape_of((hidden, width), F32), shape_of((width, hidden), F32), shape_of((width, width), F32),
              shape_of((width, 3 * width), F32)]
    return small_call(final_kernel, "finish", place_bits[0], list(parts) + recv, shapes)


def butterfly(value, bits, count):
    value = value + swap(value)
    for bit in range(bits):
        value = value + exchange(value, bit, count)
    return value


def swap(value):
    return lax.ppermute(value, "section", [(0, 1), (1, 0)])


def both(value, section):
    other = swap(value)
    first = jnp.where(section == 0, value, other)
    second = jnp.where(section == 0, other, value)
    return first, second


def body(
    images,
    cotangent,
    image_count,
    norm1_gain,
    norm1_bias,
    qkv_weight,
    query_bias,
    value_bias,
    bias_table,
    out_weight,
    out_bias,
    norm2_gain,
    norm2_bias,
    up_weight,
    up_bias,
    down_weight,
    down_bias,
):
    section = lax.axis_index("section")
    slots = images.shape[0]
    mine = slots // 2
    width = images.shape[-1]
    heads = bias_table.shape[-1]
    head_dim = width // heads
    vectors = jnp.concatenate(
        [norm1_gain, norm1_bias, query_bias, value_bias, out_bias, norm2_gain, norm2_bias, down_bias,
         up_bias.reshape(-1, width)], axis=0)
    layer_vec = both(vectors, section)
    layer_table = both(bias_table[0], section)
    layer_w = list(zip(*[both(weight[0], section) for weight in (qkv_weight, out_weight, up_weight, down_weight)]))
    perms = [jnp.asarray(window_onehot(shift), BF16) for shift in (0, SHIFT)]
    biases = [bias_tiles(layer_table[0], False), bias_tiles(layer_table[1], True)]
    base_mine = jnp.stack([section * mine, section]).astype(jnp.int32)
    base_zero = jnp.stack([section * 0, section]).astype(jnp.int32)
    live = (section * mine + jnp.arange(mine) < image_count[0]).astype(F32)
    ones = jnp.ones((mine,), F32)
    count = lax.axis_size("dp")
    bits = count.bit_length() - 1
    chip = lax.axis_index("dp")
    orders = round_orders(bits)
    place_bits = [
        jnp.stack([(chip >> order[turn]) & 1 for order in orders]).astype(jnp.int32) for turn in range(bits)
    ]

    out_zero, *kept_zero = run_forward(base_mine, images, perms[0], biases[0], layer_vec[0], layer_w[0], mine, head_dim, False)
    out_one, *kept_one = run_forward(base_zero, out_zero, perms[1], biases[1], layer_vec[1], layer_w[1], mine, head_dim, True)

    def backward(layer, base, g_rows, alive, kept):
        dres, dmix, *ffn_grads, small_ffn = run_ffn_back(base, g_rows, alive, perms[layer], layer_vec[layer], layer_w[layer], kept, mine)
        igrad, igrad_b, keep_qkv, send_qkv, tiles, small_attn = run_attn_back(
            base, perms[layer], layer_vec[layer], layer_w[layer], kept, dres, dmix, mine, head_dim)
        keep = (ffn_grads[0], ffn_grads[2], ffn_grads[4], keep_qkv)
        send = (ffn_grads[1], ffn_grads[3], ffn_grads[5], send_qkv)
        shards = reduce_shards(keep, send, orders, place_bits, count)
        return igrad, igrad_b, shards, small_ffn + small_attn, table_grad(tiles, heads)

    igrad_one, back_rows, shards_one, small_one, table_one = backward(1, base_mine, cotangent, live, kept_one)
    igrad_zero, _, shards_zero, small_zero, table_zero = backward(0, base_zero, back_rows, ones, kept_zero)

    entries = table_zero.shape[0] * heads
    pad = -entries % width
    flat = [jnp.pad(table.reshape(-1), (0, pad)).reshape(-1, width) for table in (table_zero, table_one)]
    small = jnp.stack([jnp.concatenate([small_zero, flat[0]]), jnp.concatenate([small_one, flat[1]])])
    small = butterfly(small, bits, count)
    small = jnp.where(section == 0, small[0], small[1])
    table_sum = small[SMALL_ROWS:].reshape(-1)[:entries].reshape(-1, heads)
    g_down, g_up, g_out, g_qkv = gather_layer(shards_zero, shards_one, section, orders, place_bits, count)

    def place(first, second):
        got = swap(jnp.where(section == 0, second, first))
        upper = jnp.concatenate([first, got], axis=0)
        lower = jnp.concatenate([got, second], axis=0)
        return jnp.where(section == 0, upper, lower)

    segment_out = place(out_zero, out_one)
    input_grad = place(igrad_zero, igrad_one)
    row = lambda number: small[number : number + 1]
    g_up_b = small[8 : 8 + up_bias.shape[1] // width].reshape(1, -1)
    return (
        segment_out[None], input_grad[None], row(0), row(1), g_qkv[None], row(2), row(3), table_sum[None],
        g_out[None], row(4), row(5), row(6), g_up[None], g_up_b, g_down[None], row(7),
    )


def solution(mesh):
    row = P("section", None)
    mat = P("section", None, None)
    return jax.shard_map(
        body,
        mesh=mesh,
        in_specs=(
            P("dp", None, None), P("dp", None, None), P("dp"),
            row, row, mat, row, row, mat, mat, row, row, row, mat, row, mat, row,
        ),
        out_specs=(
            P("section", "dp", None, None), P("section", "dp", None, None),
            row, row, mat, row, row, mat, mat, row, row, row, mat, row, mat, row,
        ),
        check_vma=False,
    )
```

```python
import functools

import jax
import jax.numpy as jnp
import numpy as np
from jax import lax
from jax.experimental import pallas as pl
from jax.experimental.pallas import tpu as pltpu
from jax.sharding import PartitionSpec as P


WIN = 7
SIDE = 14
SHIFT = 3
CELLS = WIN * WIN
PADW = 64
NWIN = (SIDE // WIN) ** 2
IROWS = NWIN * PADW
GROUP = 4
LANES = 128
FCHUNK = 512
EPS = 1e-05
MASKED = -100.0
PADDED = -1e30
SQRT_HALF = 0.7071067811865476
INV_ROOT_TAU = 0.3989422804014327
F32 = jnp.float32
BF16 = jnp.bfloat16
SMALL_ROWS = 16
EXTRA = 32


def window_source(offset):
    across = SIDE // WIN
    places = np.arange(SIDE * SIDE)
    window_no = places // CELLS
    cell_no = places % CELLS
    grid_row = window_no // across * WIN + cell_no // WIN
    grid_col = window_no % across * WIN + cell_no % WIN
    source = (grid_row + offset) % SIDE * SIDE + (grid_col + offset) % SIDE
    return window_no * PADW + cell_no, source


def window_onehot(offset):
    rows, source = window_source(offset)
    table = np.zeros((IROWS, SIDE * SIDE), np.float32)
    table[rows, source] = 1.0
    return table


def region_mask():
    places = np.arange(SIDE)
    labels = (places >= SIDE - WIN).astype(np.int32) + (places >= SIDE - SHIFT).astype(np.int32)
    region = (labels[:, None] * 3 + labels[None, :]).reshape(-1)
    rows, source = window_source(0)
    padded = np.full((IROWS,), -1)
    padded[rows] = region[source]
    padded = padded.reshape(NWIN, PADW)
    differ = (padded[:, :, None] != padded[:, None, :]) & (padded[:, :, None] >= 0)
    differ &= padded[:, None, :] >= 0
    return np.where(differ, MASKED, 0.0).astype(np.float32)


def relative_index():
    cells = np.arange(CELLS)
    row_of, col_of = cells // WIN, cells % WIN
    row_gap = row_of[:, None] - row_of[None, :] + WIN - 1
    return row_gap * (2 * WIN - 1) + col_of[:, None] - col_of[None, :] + WIN - 1


def pair_onehot():
    index = np.full((PADW, PADW), -1, np.int32)
    index[:CELLS, :CELLS] = relative_index().T
    entries = jnp.arange((2 * WIN - 1) ** 2)
    return (jnp.asarray(index)[:, :, None] == entries).astype(F32)


def bias_tiles(table, mask_on):
    heads = table.shape[1]
    spread = jnp.einsum("jit,th->hji", pair_onehot(), table, precision=lax.Precision.HIGHEST)
    tiles = spread.reshape(heads // GROUP, GROUP, PADW, PADW).transpose(0, 2, 1, 3)
    pad_key = np.where(np.arange(PADW) >= CELLS, PADDED, 0.0).astype(np.float32)
    tiles = tiles + pad_key[None, :, None, None]
    if mask_on:
        tiles = tiles[None] + region_mask()[:, None, :, None, :]
    else:
        tiles = tiles[None]
    return tiles.reshape(tiles.shape[0], heads // GROUP, PADW, GROUP * PADW)


def table_grad(tiles, heads):
    spread = tiles.reshape(heads // GROUP, PADW, GROUP, PADW).transpose(0, 2, 1, 3)
    spread = spread.reshape(heads, PADW, PADW)
    return jnp.einsum("jit,hji->ht", pair_onehot(), spread, precision=lax.Precision.HIGHEST)


def dot_nn(left, right):
    return lax.dot_general(left, right, (((1,), (0,)), ((), ())), preferred_element_type=F32)


def dot_nt(left, right):
    return lax.dot_general(left, right, (((1,), (1,)), ((), ())), preferred_element_type=F32)


def dot_tn(left, right):
    return lax.dot_general(left, right, (((0,), (0,)), ((), ())), preferred_element_type=F32)


def normalize(values):
    centered = values - jnp.mean(values, axis=-1, keepdims=True)
    inv_std = lax.rsqrt(jnp.mean(centered * centered, axis=-1, keepdims=True) + EPS)
    return centered * inv_std, inv_std


def norm_back(upstream, scaled, inv_std, gain):
    along = upstream * gain
    return inv_std * (
        along
        - jnp.mean(along, axis=-1, keepdims=True)
        - scaled * jnp.mean(along * scaled, axis=-1, keepdims=True)
    )


def gelu_parts(pre):
    cdf_val = 0.5 * (1.0 + lax.erf(pre * SQRT_HALF))
    density = jnp.exp(-0.5 * pre * pre) * INV_ROOT_TAU
    return pre * cdf_val, cdf_val + pre * density


def head_mask(head_dim):
    rows = lax.broadcasted_iota(jnp.int32, (GROUP * PADW, LANES), 0) // PADW
    cols = lax.broadcasted_iota(jnp.int32, (GROUP * PADW, LANES), 1) // head_dim
    return jnp.where(rows == cols, 1.0, 0.0).astype(BF16)


def expand(tile, mask):
    return jnp.concatenate([tile] * GROUP, axis=0) * mask


def collapse(wide, head_dim):
    head_of = lax.broadcasted_iota(jnp.int32, (PADW, LANES), 1) // head_dim
    total = wide[:PADW]
    for head in range(1, GROUP):
        total = jnp.where(head_of == head, wide[head * PADW : (head + 1) * PADW], total)
    return total


def rows_at(number, size):
    return pl.ds(pl.multiple_of(number * size, size), size)


def forward_kernel(
    base_ref, x_ref, perm_ref, bias_ref, vec_ref, wqkv_ref, wout_ref, wup_ref, wdown_ref,
    out_ref, xa_ref, nrm_ref, qkv_ref, prob_ref, mix_ref, res_ref, n2_ref, act_ref, slope_ref,
    *, images, head_dim, masked,
):
    width = wout_ref.shape[0]
    hidden = wup_ref.shape[1]
    groups = width // LANES
    factor = head_dim ** (-0.5)
    first = base_ref[0]

    def enter(img, carry):
        rows = rows_at(img, IROWS)
        entry = dot_nn(perm_ref[...], x_ref[first + img])
        xa_ref[rows, :] = entry.astype(BF16)
        scaled, _ = normalize(entry)
        normed = (scaled * vec_ref[0:1, :] + vec_ref[1:2, :]).astype(BF16)
        nrm_ref[rows, :] = normed
        query = (dot_nn(normed, wqkv_ref[:, :width]) + vec_ref[2:3, :]) * factor
        qkv_ref[rows, :width] = query.astype(BF16)
        qkv_ref[rows, width : 2 * width] = dot_nn(normed, wqkv_ref[:, width : 2 * width]).astype(BF16)
        value = dot_nn(normed, wqkv_ref[:, 2 * width :]) + vec_ref[3:4, :]
        qkv_ref[rows, 2 * width :] = value.astype(BF16)
        return carry

    lax.fori_loop(0, images, enter, 0)
    mask = head_mask(head_dim)

    def attend(win, carry):
        rows = rows_at(win, PADW)
        bias_no = win % NWIN if masked else 0
        for grp in range(groups):
            at = grp * LANES
            query = qkv_ref[rows, at : at + LANES]
            key = qkv_ref[rows, width + at : width + at + LANES]
            value = qkv_ref[rows, 2 * width + at : 2 * width + at + LANES]
            score = dot_nt(key, expand(query, mask)) + bias_ref[bias_no, grp]
            expo = jnp.exp(score - jnp.max(score, axis=0, keepdims=True))
            prob = expo * (1.0 / jnp.sum(expo, axis=0, keepdims=True))
            prob_ref[win, grp] = prob
            wide = dot_tn(prob.astype(BF16), value)
            mix_ref[rows, at : at + LANES] = collapse(wide, head_dim).astype(BF16)
        return carry

    lax.fori_loop(0, images * NWIN, attend, 0)

    def leave(img, carry):
        rows = rows_at(img, IROWS)
        entry = xa_ref[rows, :].astype(F32)
        resid = entry + dot_nn(mix_ref[rows, :], wout_ref[...]) + vec_ref[4:5, :]
        res_ref[rows, :] = resid
        scaled, _ = normalize(resid)
        n2_ref[rows, :] = (scaled * vec_ref[5:6, :] + vec_ref[6:7, :]).astype(BF16)
        for part in range(hidden // FCHUNK):
            at = part * FCHUNK
            pre = dot_nn(n2_ref[rows, :], wup_ref[:, at : at + FCHUNK]) + vec_ref[8 + part : 9 + part, :]
            activ, slope = gelu_parts(pre)
            act_ref[rows, at : at + FCHUNK] = activ.astype(BF16)
            slope_ref[rows, at : at + FCHUNK] = slope
        done = res_ref[rows, :] + dot_nn(act_ref[rows, :], wdown_ref[...]) + vec_ref[7:8, :]
        out_ref[img] = dot_tn(perm_ref[...], done.astype(BF16)).astype(BF16)
        return carry

    lax.fori_loop(0, images, leave, 0)


def ffn_back_kernel(
    base_ref, g_ref, live_ref, perm_ref, vec_ref, wout_ref, wup_ref, wdown_ref,
    mix_ref, res_ref, n2_ref, act_ref, slope_ref,
    dres_ref, dmix_ref, keep_ref, send_ref,
    small_ref, gb_ref, dpre_ref, dresb_ref,
    *, images,
):
    width = wout_ref.shape[0]
    hidden = wup_ref.shape[1]
    first = base_ref[0]
    section = base_ref[1]
    small_ref[...] = jnp.zeros_like(small_ref)

    def step(img, carry):
        rows = rows_at(img, IROWS)
        upstream = dot_nn(perm_ref[...], g_ref[first + img]) * live_ref[img]
        gb_ref[rows, :] = upstream.astype(BF16)
        small_ref[7:8, :] += jnp.sum(upstream, axis=0, keepdims=True)
        for part in range(hidden // FCHUNK):
            at = part * FCHUNK
            dpre = dot_nt(gb_ref[rows, :], wdown_ref[at : at + FCHUNK, :]) * slope_ref[rows, at : at + FCHUNK]
            small_ref[8 + part : 9 + part, :] += jnp.sum(dpre, axis=0, keepdims=True)
            dpre_ref[rows, at : at + FCHUNK] = dpre.astype(BF16)
        dnorm = dot_nt(dpre_ref[rows, :], wup_ref[...])
        scaled, inv_std = normalize(res_ref[rows, :])
        small_ref[5:6, :] += jnp.sum(dnorm * scaled, axis=0, keepdims=True)
        small_ref[6:7, :] += jnp.sum(dnorm, axis=0, keepdims=True)
        dres = gb_ref[rows, :].astype(F32) + norm_back(dnorm, scaled, inv_std, vec_ref[5:6, :])
        dres_ref[rows, :] = dres
        small_ref[4:5, :] += jnp.sum(dres, axis=0, keepdims=True)
        dresb_ref[rows, :] = dres.astype(BF16)
        dmix_ref[rows, :] = dot_nt(dresb_ref[rows, :], wout_ref[...]).astype(BF16)
        return carry

    lax.fori_loop(0, images, step, 0)
    span = hidden // 2
    for side, dest in ((0, keep_ref), (1, send_ref)):
        half = section if side == 0 else 1 - section
        for part in range(span // FCHUNK):
            cols = pl.ds(pl.multiple_of(half * span + part * FCHUNK, FCHUNK), FCHUNK)
            dest[part * FCHUNK : (part + 1) * FCHUNK, :] = dot_tn(act_ref[:, cols], gb_ref[...]).astype(BF16)
        cols = rows_at(half, width // 2)
        for part in range(hidden // width):
            at = part * width
            block = dot_tn(n2_ref[:, cols], dpre_ref[:, at : at + width])
            dest[span + part * (width // 2) : span + (part + 1) * (width // 2), :] = block.astype(BF16)
        dest[2 * span :, :] = dot_tn(mix_ref[:, cols], dresb_ref[...]).astype(BF16)


def attn_back_kernel(
    base_ref, perm_ref, vec_ref, wqkv_ref, xa_ref, nrm_ref, qkv_ref, prob_ref, dres_ref, dmix_ref,
    igrad_ref, igrad_b_ref, keep_ref, send_ref, tiles_ref, small_ref, dqkv_ref,
    *, images, head_dim,
):
    width = wqkv_ref.shape[0]
    groups = width // LANES
    factor = head_dim ** (-0.5)
    section = base_ref[1]
    small_ref[...] = jnp.zeros_like(small_ref)
    tiles_ref[...] = jnp.zeros_like(tiles_ref)
    mask = head_mask(head_dim)

    def attend(win, carry):
        rows = rows_at(win, PADW)
        for grp in range(groups):
            at = grp * LANES
            query = qkv_ref[rows, at : at + LANES]
            key = qkv_ref[rows, width + at : width + at + LANES]
            value = qkv_ref[rows, 2 * width + at : 2 * width + at + LANES]
            dmix = expand(dmix_ref[rows, at : at + LANES], mask)
            prob = prob_ref[win, grp]
            dprob = dot_nt(value, dmix)
            dvalue = dot_nn(prob.astype(BF16), dmix)
            dscore = prob * (dprob - jnp.sum(prob * dprob, axis=0, keepdims=True))
            tiles_ref[grp] += dscore
            dscore_b = dscore.astype(BF16)
            dkey = dot_nn(dscore_b, expand(query, mask))
            dquery = collapse(dot_tn(dscore_b, key), head_dim) * factor
            small_ref[2:3, at : at + LANES] += jnp.sum(dquery, axis=0, keepdims=True)
            small_ref[3:4, at : at + LANES] += jnp.sum(dvalue, axis=0, keepdims=True)
            dqkv_ref[rows, at : at + LANES] = dquery.astype(BF16)
            dqkv_ref[rows, width + at : width + at + LANES] = dkey.astype(BF16)
            dqkv_ref[rows, 2 * width + at : 2 * width + at + LANES] = dvalue.astype(BF16)
        return carry

    lax.fori_loop(0, images * NWIN, attend, 0)

    def leave(img, carry):
        rows = rows_at(img, IROWS)
        dnorm = dot_nt(dqkv_ref[rows, :], wqkv_ref[...])
        scaled, inv_std = normalize(xa_ref[rows, :].astype(F32))
        small_ref[0:1, :] += jnp.sum(dnorm * scaled, axis=0, keepdims=True)
        small_ref[1:2, :] += jnp.sum(dnorm, axis=0, keepdims=True)
        grad = dres_ref[rows, :] + norm_back(dnorm, scaled, inv_std, vec_ref[0:1, :])
        high = grad.astype(BF16)
        low = (grad - high.astype(F32)).astype(BF16)
        moved = dot_tn(perm_ref[...], high)
        igrad_b_ref[img] = moved.astype(BF16)
        igrad_ref[img] = moved + dot_tn(perm_ref[...], low)
        return carry

    lax.fori_loop(0, images, leave, 0)
    for side, dest in ((0, keep_ref), (1, send_ref)):
        half = section if side == 0 else 1 - section
        cols = rows_at(half, width // 2)
        for part in range(3):
            at = part * width
            block = dot_tn(nrm_ref[:, cols], dqkv_ref[:, at : at + width])
            dest[part * (width // 2) : (part + 1) * (width // 2), :] = block.astype(BF16)


def vmem():
    return pl.BlockSpec(memory_space=pltpu.VMEM)


def smem():
    return pl.BlockSpec(memory_space=pltpu.SMEM)


def shape_of(shape, dtype):
    return jax.ShapeDtypeStruct(shape, dtype)


PARAMS = pltpu.CompilerParams(vmem_limit_bytes=30 * 1024 * 1024)
SMALL_PARAMS = pltpu.CompilerParams(vmem_limit_bytes=24 * 1024 * 1024)


def run_forward(base, rows_in, perm, bias, vec, weights, images, head_dim, masked):
    wqkv, wout, wup, wdown = weights
    width, hidden = wup.shape
    total = images * IROWS
    shapes = (
        shape_of((images, SIDE * SIDE, width), BF16),
        shape_of((total, width), BF16),
        shape_of((total, width), BF16),
        shape_of((total, 3 * width), BF16),
        shape_of((images * NWIN, width // LANES, PADW, GROUP * PADW), F32),
        shape_of((total, width), BF16),
        shape_of((total, width), F32),
        shape_of((total, width), BF16),
        shape_of((total, hidden), BF16),
        shape_of((total, hidden), F32),
    )
    return pl.pallas_call(
        functools.partial(forward_kernel, images=images, head_dim=head_dim, masked=masked),
        out_shape=shapes,
        in_specs=[smem()] + [vmem()] * 8,
        out_specs=tuple(vmem() for _ in shapes),
        compiler_params=PARAMS,
        name="layer_forward",
    )(base, rows_in, perm, bias, vec, wqkv, wout, wup, wdown)


def run_ffn_back(base, g_rows, live, perm, vec, weights, kept, images):
    _, wout, wup, wdown = weights
    _, _, _, _, mix, res, n2, act, slope = kept
    width, hidden = wup.shape
    total = images * IROWS
    shapes = (
        shape_of((total, width), F32),
        shape_of((total, width), BF16),
        shape_of((hidden + width // 2, width), BF16),
        shape_of((hidden + width // 2, width), BF16),
        shape_of((SMALL_ROWS, width), F32),
    )
    return pl.pallas_call(
        functools.partial(ffn_back_kernel, images=images),
        out_shape=shapes,
        in_specs=[smem(), vmem(), smem()] + [vmem()] * 10,
        out_specs=tuple(vmem() for _ in shapes),
        scratch_shapes=[
            pltpu.VMEM((total, width), BF16),
            pltpu.VMEM((total, hidden), BF16),
            pltpu.VMEM((total, width), BF16),
        ],
        compiler_params=PARAMS,
        name="ffn_back",
    )(base, g_rows, live, perm, vec, wout, wup, wdown, mix, res, n2, act, slope)


def run_attn_back(base, perm, vec, weights, kept, dres, dmix, images, head_dim):
    wqkv = weights[0]
    xa, nrm, qkv, prob = kept[:4]
    width = wqkv.shape[0]
    total = images * IROWS
    shapes = (
        shape_of((images, SIDE * SIDE, width), F32),
        shape_of((images, SIDE * SIDE, width), BF16),
        shape_of((3 * width // 2, width), BF16),
        shape_of((3 * width // 2, width), BF16),
        shape_of((width // LANES, PADW, GROUP * PADW), F32),
        shape_of((SMALL_ROWS, width), F32),
    )
    return pl.pallas_call(
        functools.partial(attn_back_kernel, images=images, head_dim=head_dim),
        out_shape=shapes,
        in_specs=[smem()] + [vmem()] * 9,
        out_specs=tuple(vmem() for _ in shapes),
        scratch_shapes=[pltpu.VMEM((total, 3 * width), BF16)],
        compiler_params=PARAMS,
        name="attn_back",
    )(base, perm, vec, wqkv, xa, nrm, qkv, prob, dres, dmix)


def round_orders(bits):
    if bits == 4:
        return ((0, 1, 2, 3), (1, 0, 3, 2), (2, 3, 0, 1), (3, 2, 0, 1))
    axes = list(range(bits))
    return tuple(tuple(axes[turn:] + axes[:turn]) for turn in range(4))


def added(left, right):
    return (left.astype(F32) + right.astype(F32)).astype(BF16)


def first_ffn_kernel(bit_ref, keep_ref, recv_ref, *outs, turn):
    tail_ref = outs[4]
    for color in range(2):
        half = outs[color].shape[0]
        bit = bit_ref[turn + color]
        for side, place in ((0, bit), (2, 1 - bit)):
            rows = pl.ds(pl.multiple_of(color * 2 * half + place * half, half), half)
            outs[side + color][...] = added(keep_ref[rows, :], recv_ref[rows, :])
    tail = keep_ref.shape[0] - tail_ref.shape[0]
    tail_ref[...] = added(keep_ref[tail:, :], recv_ref[tail:, :])


def first_qkv_kernel(bit_ref, tail_ref, keep_ref, recv_ref, *outs, turn):
    half = outs[0].shape[0]
    head = added(keep_ref[:half, :], recv_ref[:half, :])
    low = bit_ref[turn + 2] == 0
    outs[0][...] = jnp.where(low, tail_ref[...], head)
    outs[2][...] = jnp.where(low, head, tail_ref[...])
    bit = bit_ref[turn + 3]
    for side, place in ((1, bit), (3, 1 - bit)):
        rows = pl.ds(pl.multiple_of(half + place * half, half), half)
        outs[side][...] = added(keep_ref[rows, :], recv_ref[rows, :])


def sum_kernel(bit_ref, *refs, turn):
    keep, recv, outs = refs[:4], refs[4:8], refs[8:]
    for color in range(4):
        half = keep[color].shape[0] // 2
        bit = bit_ref[turn + color]
        for side, start in ((0, bit * half), (4, (1 - bit) * half)):
            rows = pl.ds(pl.multiple_of(start, 8), half)
            outs[side + color][...] = added(keep[color][rows, :], recv[color][rows, :])


def last_kernel(bit_ref, *refs, turn):
    keep, recv, out_ref = refs[:4], refs[4:8], refs[8]
    at = 0
    for color in range(4):
        size = keep[color].shape[0]
        out_ref[at : at + size, :] = added(keep[color][...], recv[color][...])
        at += size


def split_small(value):
    high = value.astype(BF16)
    return high, (value - high.astype(F32)).astype(BF16)


def pick_kernel(section_ref, zero_ref, one_ref, small_zero_ref, small_one_ref, own_ref, send_ref, *, turn):
    first = section_ref[0] == 0
    size = zero_ref.shape[0]
    own_ref[:size, :] = jnp.where(first, zero_ref[...], one_ref[...])
    send_ref[:size, :] = jnp.where(first, one_ref[...], zero_ref[...])
    for dest, value in (
        (own_ref, jnp.where(first, small_zero_ref[...], small_one_ref[...])),
        (send_ref, jnp.where(first, small_one_ref[...], small_zero_ref[...])),
    ):
        high, low = split_small(value)
        dest[size : size + EXTRA, :] = high
        dest[size + EXTRA :, :] = low


def join_kernel(section_ref, own_ref, got_ref, *outs, turn):
    first = section_ref[0] == 0
    at = 0
    for color in range(4):
        size = outs[color].shape[1] - (EXTRA if color == 3 else 0)
        mine, other = own_ref[at : at + size, :], got_ref[at : at + size, :]
        outs[color][0, :size, :] = jnp.where(first, mine, other)
        outs[color][1, :size, :] = jnp.where(first, other, mine)
        at += size
    total = jnp.zeros((EXTRA, own_ref.shape[1]), F32)
    for ref in (own_ref, got_ref):
        total += ref[at : at + EXTRA, :].astype(F32) + ref[at + EXTRA :, :].astype(F32)
    high, low = split_small(total)
    outs[3][0, size:, :] = high
    outs[3][1, size:, :] = low


def small_total(own_ref, recv_ref):
    total = jnp.zeros((EXTRA, own_ref.shape[2]), F32)
    at = own_ref.shape[1] - EXTRA
    for ref in (own_ref, recv_ref):
        total += ref[0, at:, :].astype(F32) + ref[1, at:, :].astype(F32)
    return total


def merge_kernel(bit_ref, *refs, turn):
    own, recv, outs = refs[:4], refs[4:8], refs[8:]
    for color in range(4):
        size = own[color].shape[1] - (EXTRA if color == 3 else 0)
        bit = bit_ref[turn + color]
        outs[color][:, pl.ds(pl.multiple_of(bit * size, 8), size), :] = own[color][:, :size, :]
        outs[color][:, pl.ds(pl.multiple_of((1 - bit) * size, 8), size), :] = recv[color][:, :size, :]
    high, low = split_small(small_total(own[3], recv[3]))
    outs[3][0, 2 * size :, :] = high
    outs[3][1, 2 * size :, :] = low


def final_kernel(bit_ref, *refs, turn):
    own, recv = refs[:4], refs[4:8]
    down_ref, up_ref, out_ref, qkv_ref = refs[8:12]
    rows_refs, up_bias_ref, table_ref = refs[12:20], refs[20], refs[21]
    width = out_ref.shape[1]
    part = width // 2
    for half in range(2):
        rows = slice(half * part, (half + 1) * part)
        bit = bit_ref[turn + 0]
        span = own[0].shape[1]
        for side, source in ((bit, own[0]), (1 - bit, recv[0])):
            down_ref[pl.ds(pl.multiple_of(half * 2 * span + side * span, span), span), :] = source[half].astype(F32)
        bit = bit_ref[turn + 1]
        blocks = own[1].shape[1] // part
        for side, source in ((bit, own[1]), (1 - bit, recv[1])):
            for block in range(blocks):
                cols = pl.ds(pl.multiple_of((side * blocks + block) * width, width), width)
                up_ref[rows, cols] = source[half, block * part : (block + 1) * part, :].astype(F32)
        is_low = bit_ref[turn + 2] == 0
        mine, other = own[2][half].astype(F32), recv[2][half].astype(F32)
        out_ref[rows, :] = jnp.where(is_low, mine, other)
        qkv_ref[rows, :width] = jnp.where(is_low, other, mine)
        bit = bit_ref[turn + 3]
        size = own[3].shape[1] - EXTRA
        for side, source in ((bit, own[3]), (1 - bit, recv[3])):
            cols = pl.ds(pl.multiple_of((1 + side) * width, width), width)
            qkv_ref[rows, cols] = source[half, :size, :].astype(F32)
    total = small_total(own[3], recv[3])
    for number, ref in enumerate(rows_refs):
        ref[...] = total[number : number + 1, :]
    for block in range(up_bias_ref.shape[1] // width):
        up_bias_ref[:, block * width : (block + 1) * width] = total[8 + block : 9 + block, :]
    table_ref[...] = total[SMALL_ROWS:, : table_ref.shape[1]]


def small_call(kernel, bits, arrays, shapes, turn=0):
    return pl.pallas_call(
        functools.partial(kernel, turn=4 * turn),
        out_shape=tuple(shapes),
        in_specs=[smem()] + [vmem()] * len(arrays),
        out_specs=tuple(vmem() for _ in shapes),
        compiler_params=SMALL_PARAMS,
    )(bits, *arrays)


def exchange(value, bit, count):
    return lax.ppermute(value, "dp", [(one, one ^ (1 << bit)) for one in range(count)])


def start_rounds(keep_ffn, send_ffn, keep_qkv, send_qkv, place_bits):
    width = keep_ffn.shape[1]
    recv_ffn = swap(send_ffn)
    recv_qkv = swap(send_qkv)
    long = shape_of(((keep_ffn.shape[0] - width // 2) // 4, width), BF16)
    short = shape_of((width // 2, width), BF16)
    *ffn, tail = small_call(first_ffn_kernel, place_bits, (keep_ffn, recv_ffn), [long] * 4 + [short])
    rest = small_call(first_qkv_kernel, place_bits, (tail, keep_qkv, recv_qkv), [short] * 4)
    return (*ffn[:2], *rest[:2], *ffn[2:], *rest[2:])


def reduce_rounds(parts, orders, place_bits, count):
    width = parts[0].shape[1]
    rounds = len(orders[0])
    for turn in range(rounds):
        mine, gone = parts[:4], parts[4:]
        recv = [exchange(part, order[turn], count) for part, order in zip(gone, orders)]
        if turn + 1 < rounds:
            halves = [shape_of((part.shape[0] // 2, width), BF16) for part in mine]
            parts = small_call(sum_kernel, place_bits, list(mine) + recv, halves * 2, turn + 1)
        else:
            total = shape_of((sum(part.shape[0] for part in mine), width), BF16)
            parts = small_call(last_kernel, place_bits, list(mine) + recv, [total])
    return parts[0]


def gather_layer(shard_zero, shard_one, small_zero, small_one, where, sizes, hidden, entries, heads, orders, place_bits, count):
    rows, width = shard_zero.shape
    both_shape = [shape_of((rows + 2 * EXTRA, width), BF16)] * 2
    own, send = small_call(pick_kernel, where, (shard_zero, shard_one, small_zero, small_one), both_shape)
    got = swap(send)
    extras = (0, 0, 0, EXTRA)
    shapes = [shape_of((2, size + extra, width), BF16) for size, extra in zip(sizes, extras)]
    parts = small_call(join_kernel, where, (own, got), shapes)
    rounds = len(orders[0])
    for turn in reversed(range(rounds)):
        recv = [exchange(part, order[turn], count) for part, order in zip(parts, orders)]
        if turn:
            shapes = [
                shape_of((2, 2 * part.shape[1] - extra, width), BF16) for part, extra in zip(parts, extras)
            ]
            parts = small_call(merge_kernel, place_bits, list(parts) + recv, shapes, turn)
    shapes = [shape_of((hidden, width), F32), shape_of((width, hidden), F32), shape_of((width, width), F32),
              shape_of((width, 3 * width), F32)]
    shapes += [shape_of((1, width), F32)] * 8 + [shape_of((1, hidden), F32), shape_of((heads, entries), F32)]
    return small_call(final_kernel, place_bits, list(parts) + recv, shapes)


def swap(value):
    return lax.ppermute(value, "section", [(0, 1), (1, 0)])


def both(value, section):
    other = swap(value)
    first = jnp.where(section == 0, value, other)
    second = jnp.where(section == 0, other, value)
    return first, second


def body(
    images,
    cotangent,
    image_count,
    norm1_gain,
    norm1_bias,
    qkv_weight,
    query_bias,
    value_bias,
    bias_table,
    out_weight,
    out_bias,
    norm2_gain,
    norm2_bias,
    up_weight,
    up_bias,
    down_weight,
    down_bias,
):
    section = lax.axis_index("section")
    slots = images.shape[0]
    mine = slots // 2
    width = images.shape[-1]
    heads = bias_table.shape[-1]
    head_dim = width // heads
    vectors = jnp.concatenate(
        [norm1_gain, norm1_bias, query_bias, value_bias, out_bias, norm2_gain, norm2_bias, down_bias,
         up_bias.reshape(-1, width)], axis=0)
    layer_vec = both(vectors, section)
    layer_table = both(bias_table[0], section)
    layer_w = list(zip(*[both(weight[0], section) for weight in (qkv_weight, out_weight, up_weight, down_weight)]))
    perms = [jnp.asarray(window_onehot(shift), BF16) for shift in (0, SHIFT)]
    biases = [bias_tiles(layer_table[0], False), bias_tiles(layer_table[1], True)]
    base_mine = jnp.stack([section * mine, section]).astype(jnp.int32)
    base_zero = jnp.stack([section * 0, section]).astype(jnp.int32)
    live = (section * mine + jnp.arange(mine) < image_count[0]).astype(F32)
    ones = jnp.ones((mine,), F32)
    count = lax.axis_size("dp")
    bits = count.bit_length() - 1
    chip = lax.axis_index("dp")
    orders = round_orders(bits)
    turns = np.array([[order[turn] for order in orders] for turn in range(bits)]).reshape(-1)
    place_bits = (chip >> turns.astype(np.int32)) & 1

    out_zero, *kept_zero = run_forward(base_mine, images, perms[0], biases[0], layer_vec[0], layer_w[0], mine, head_dim, False)
    out_one, *kept_one = run_forward(base_zero, out_zero, perms[1], biases[1], layer_vec[1], layer_w[1], mine, head_dim, True)

    def backward(layer, base, g_rows, alive, kept):
        dres, dmix, keep_ffn, send_ffn, small_ffn = run_ffn_back(
            base, g_rows, alive, perms[layer], layer_vec[layer], layer_w[layer], kept, mine)
        igrad, igrad_b, keep_qkv, send_qkv, tiles, small_attn = run_attn_back(
            base, perms[layer], layer_vec[layer], layer_w[layer], kept, dres, dmix, mine, head_dim)
        parts = start_rounds(keep_ffn, send_ffn, keep_qkv, send_qkv, place_bits)
        shard = reduce_rounds(parts, orders, place_bits, count)
        table = table_grad(tiles, heads)
        table = jnp.pad(table, ((0, 0), (0, width - table.shape[1])))
        return igrad, igrad_b, shard, jnp.concatenate([small_ffn + small_attn, table]), [part.shape[0] for part in parts[:4]]

    igrad_one, back_rows, shard_one, small_one, halves = backward(1, base_mine, cotangent, live, kept_one)
    igrad_zero, _, shard_zero, small_zero, _ = backward(0, base_zero, back_rows, ones, kept_zero)

    hidden = up_bias.shape[1]
    sizes = [half >> (bits - 1) for half in halves]
    where = section.astype(jnp.int32).reshape(1)
    g_down, g_up, g_out, g_qkv, *vecs, g_up_b, g_table = gather_layer(
        shard_zero, shard_one, small_zero, small_one, where, sizes, hidden, bias_table.shape[1], heads, orders,
        place_bits, count)

    def place(first, second):
        got = swap(jnp.where(section == 0, second, first))
        upper = jnp.concatenate([first, got], axis=0)
        lower = jnp.concatenate([got, second], axis=0)
        return jnp.where(section == 0, upper, lower)

    segment_out = place(out_zero, out_one)
    input_grad = place(igrad_zero, igrad_one)
    g_gain_one, g_bias_one, g_query, g_value, g_out_b, g_gain_two, g_bias_two, g_down_b = vecs
    return (
        segment_out[None], input_grad[None], g_gain_one, g_bias_one, g_qkv[None], g_query, g_value, g_table.T[None],
        g_out[None], g_out_b, g_gain_two, g_bias_two, g_up[None], g_up_b, g_down[None], g_down_b,
    )


def solution(mesh):
    row = P("section", None)
    mat = P("section", None, None)

    return jax.shard_map(
        body,
        mesh=mesh,
        in_specs=(
            P("dp", None, None), P("dp", None, None), P("dp"),
            row, row, mat, row, row, mat, mat, row, row, row, mat, row, mat, row,
        ),
        out_specs=(
            P("section", "dp", None, None), P("section", "dp", None, None),
            row, row, mat, row, row, mat, mat, row, row, row, mat, row, mat, row,
        ),
        check_vma=False,
    )
```

```python
import functools

import jax
import jax.numpy as jnp
import numpy as np
from jax import lax
from jax.experimental import pallas as pl
from jax.experimental.pallas import tpu as pltpu
from jax.sharding import PartitionSpec as P


WIN = 7
SIDE = 14
SHIFT = 3
CELLS = WIN * WIN
PADW = 64
NWIN = (SIDE // WIN) ** 2
IROWS = NWIN * PADW
GROUP = 4
LANES = 128
FCHUNK = 512
EPS = 1e-05
MASKED = -100.0
PADDED = -1e30
SQRT_HALF = 0.7071067811865476
INV_ROOT_TAU = 0.3989422804014327
F32 = jnp.float32
BF16 = jnp.bfloat16
SMALL_ROWS = 16
EXTRA = 32


def window_source(offset):
    across = SIDE // WIN
    places = np.arange(SIDE * SIDE)
    window_no = places // CELLS
    cell_no = places % CELLS
    grid_row = window_no // across * WIN + cell_no // WIN
    grid_col = window_no % across * WIN + cell_no % WIN
    source = (grid_row + offset) % SIDE * SIDE + (grid_col + offset) % SIDE
    return window_no * PADW + cell_no, source


def window_onehot(offset):
    rows, source = window_source(offset)
    table = np.zeros((IROWS, SIDE * SIDE), np.float32)
    table[rows, source] = 1.0
    return table


def region_mask():
    places = np.arange(SIDE)
    labels = (places >= SIDE - WIN).astype(np.int32) + (places >= SIDE - SHIFT).astype(np.int32)
    region = (labels[:, None] * 3 + labels[None, :]).reshape(-1)
    rows, source = window_source(0)
    padded = np.full((IROWS,), -1)
    padded[rows] = region[source]
    padded = padded.reshape(NWIN, PADW)
    differ = (padded[:, :, None] != padded[:, None, :]) & (padded[:, :, None] >= 0)
    differ &= padded[:, None, :] >= 0
    return np.where(differ, MASKED, 0.0).astype(np.float32)


def relative_index():
    cells = np.arange(CELLS)
    row_of, col_of = cells // WIN, cells % WIN
    row_gap = row_of[:, None] - row_of[None, :] + WIN - 1
    return row_gap * (2 * WIN - 1) + col_of[:, None] - col_of[None, :] + WIN - 1


def pair_onehot():
    index = np.full((PADW, PADW), -1, np.int32)
    index[:CELLS, :CELLS] = relative_index().T
    entries = lax.broadcasted_iota(jnp.int32, ((2 * WIN - 1) ** 2, PADW * PADW), 0)
    return (entries == jnp.asarray(index.reshape(1, -1))).astype(BF16)


def three_terms(value):
    high = lax.reduce_precision(value, 8, 7)
    mid = lax.reduce_precision(value - high, 8, 7)
    return jnp.stack([high, mid, value - high - mid]).astype(BF16)


def bias_tiles(tables, onehot):
    layers, _, heads = tables.shape
    terms = three_terms(tables.transpose(0, 2, 1)).reshape(3 * layers * heads, -1)
    spread = dot_nn(terms, onehot).reshape(3, layers * heads, -1).sum(axis=0)
    tiles = spread.reshape(layers, heads // GROUP, GROUP, PADW, PADW).transpose(0, 1, 3, 2, 4)
    pad_key = np.where(np.arange(PADW) >= CELLS, PADDED, 0.0).astype(np.float32)
    tiles = tiles + pad_key[None, None, :, None, None]
    plain = tiles[0][None]
    masked = tiles[1][None] + region_mask()[:, None, :, None, :]
    return [part.reshape(part.shape[0], heads // GROUP, PADW, GROUP * PADW) for part in (plain, masked)]


def table_grad(tiles, heads, onehot):
    spread = tiles.reshape(heads // GROUP, PADW, GROUP, PADW).transpose(0, 2, 1, 3)
    terms = three_terms(spread.reshape(heads, PADW * PADW)).reshape(3 * heads, -1)
    return dot_nt(terms, onehot).reshape(3, heads, -1).sum(axis=0)


def dot_nn(left, right):
    return lax.dot_general(left, right, (((1,), (0,)), ((), ())), preferred_element_type=F32)


def dot_nt(left, right):
    return lax.dot_general(left, right, (((1,), (1,)), ((), ())), preferred_element_type=F32)


def dot_tn(left, right):
    return lax.dot_general(left, right, (((0,), (0,)), ((), ())), preferred_element_type=F32)


def normalize(values):
    centered = values - jnp.mean(values, axis=-1, keepdims=True)
    inv_std = lax.rsqrt(jnp.mean(centered * centered, axis=-1, keepdims=True) + EPS)
    return centered * inv_std, inv_std


def norm_back(upstream, scaled, inv_std, gain):
    along = upstream * gain
    return inv_std * (
        along
        - jnp.mean(along, axis=-1, keepdims=True)
        - scaled * jnp.mean(along * scaled, axis=-1, keepdims=True)
    )


def gelu_parts(pre):
    cdf_val = 0.5 * (1.0 + lax.erf(pre * SQRT_HALF))
    density = jnp.exp(-0.5 * pre * pre) * INV_ROOT_TAU
    return pre * cdf_val, cdf_val + pre * density


def head_mask(head_dim):
    rows = lax.broadcasted_iota(jnp.int32, (GROUP * PADW, LANES), 0) // PADW
    cols = lax.broadcasted_iota(jnp.int32, (GROUP * PADW, LANES), 1) // head_dim
    return jnp.where(rows == cols, 1.0, 0.0).astype(BF16)


def expand(tile, mask):
    return jnp.concatenate([tile] * GROUP, axis=0) * mask


def collapse(wide, head_dim):
    head_of = lax.broadcasted_iota(jnp.int32, (PADW, LANES), 1) // head_dim
    total = wide[:PADW]
    for head in range(1, GROUP):
        total = jnp.where(head_of == head, wide[head * PADW : (head + 1) * PADW], total)
    return total


def rows_at(number, size):
    return pl.ds(pl.multiple_of(number * size, size), size)


def forward_kernel(
    base_ref, x_ref, perm_ref, bias_ref, vec_ref, wqkv_ref, wout_ref, wup_ref, wdown_ref,
    out_ref, *refs, images, head_dim, masked, spill,
):
    kept = refs[9:18] if spill else refs
    xa_ref, nrm_ref, qkv_ref, prob_ref, mix_ref, res_ref, n2_ref, act_ref, slope_ref = kept

    def whole_copy(number):
        return pltpu.make_async_copy(kept[number], refs[number], refs[18].at[number])

    def image_copy(number, img):
        rows = rows_at(img, IROWS)
        return pltpu.make_async_copy(kept[number].at[rows, :], refs[number].at[rows, :], refs[19].at[number, img])

    width = wout_ref.shape[0]
    hidden = wup_ref.shape[1]
    groups = width // LANES
    factor = head_dim ** (-0.5)
    first = base_ref[0]

    def enter(img, carry):
        rows = rows_at(img, IROWS)
        entry = dot_nn(perm_ref[...], x_ref[first + img])
        xa_ref[rows, :] = entry.astype(BF16)
        scaled, _ = normalize(entry)
        normed = (scaled * vec_ref[0:1, :] + vec_ref[1:2, :]).astype(BF16)
        nrm_ref[rows, :] = normed
        query = (dot_nn(normed, wqkv_ref[:, :width]) + vec_ref[2:3, :]) * factor
        qkv_ref[rows, :width] = query.astype(BF16)
        qkv_ref[rows, width : 2 * width] = dot_nn(normed, wqkv_ref[:, width : 2 * width]).astype(BF16)
        value = dot_nn(normed, wqkv_ref[:, 2 * width :]) + vec_ref[3:4, :]
        qkv_ref[rows, 2 * width :] = value.astype(BF16)
        return carry

    lax.fori_loop(0, images, enter, 0)
    if spill:
        for number in range(3):
            whole_copy(number).start()
    mask = head_mask(head_dim)

    def attend(win, carry):
        rows = rows_at(win, PADW)
        bias_no = win % NWIN if masked else 0
        for grp in range(groups):
            at = grp * LANES
            query = qkv_ref[rows, at : at + LANES]
            key = qkv_ref[rows, width + at : width + at + LANES]
            value = qkv_ref[rows, 2 * width + at : 2 * width + at + LANES]
            score = dot_nt(key, expand(query, mask)) + bias_ref[bias_no, grp]
            expo = jnp.exp(score - jnp.max(score, axis=0, keepdims=True))
            prob = expo * (1.0 / jnp.sum(expo, axis=0, keepdims=True))
            prob_ref[win, grp] = prob
            wide = dot_tn(prob.astype(BF16), value)
            mix_ref[rows, at : at + LANES] = collapse(wide, head_dim).astype(BF16)
        return carry

    lax.fori_loop(0, images * NWIN, attend, 0)
    if spill:
        for number in range(3, 5):
            whole_copy(number).start()

    def leave(img, carry):
        rows = rows_at(img, IROWS)
        entry = xa_ref[rows, :].astype(F32)
        resid = entry + dot_nn(mix_ref[rows, :], wout_ref[...]) + vec_ref[4:5, :]
        res_ref[rows, :] = resid
        scaled, _ = normalize(resid)
        n2_ref[rows, :] = (scaled * vec_ref[5:6, :] + vec_ref[6:7, :]).astype(BF16)
        for part in range(hidden // FCHUNK):
            at = part * FCHUNK
            pre = dot_nn(n2_ref[rows, :], wup_ref[:, at : at + FCHUNK]) + vec_ref[8 + part : 9 + part, :]
            activ, slope = gelu_parts(pre)
            act_ref[rows, at : at + FCHUNK] = activ.astype(BF16)
            slope_ref[rows, at : at + FCHUNK] = slope.astype(BF16)
        done = res_ref[rows, :] + dot_nn(act_ref[rows, :], wdown_ref[...]) + vec_ref[7:8, :]
        out_ref[img] = dot_tn(perm_ref[...], done.astype(BF16)).astype(BF16)
        if spill:
            for number in range(5, 9):
                image_copy(number, img).start()
        return carry

    lax.fori_loop(0, images, leave, 0)
    if spill:
        for number in range(5):
            whole_copy(number).wait()
        for img in range(images):
            for number in range(5, 9):
                image_copy(number, img).wait()


def ffn_back_kernel(
    base_ref, g_ref, live_ref, perm_ref, vec_ref, wout_ref, wup_ref, wdown_ref,
    mix_ref, res_ref, n2_ref, act_ref, slope_ref,
    dres_ref, dmix_ref, keep_ref, send_ref,
    small_ref, gb_ref, dpre_ref, dresb_ref,
    *, images,
):
    width = wout_ref.shape[0]
    hidden = wup_ref.shape[1]
    first = base_ref[0]
    section = base_ref[1]
    small_ref[...] = jnp.zeros_like(small_ref)

    def step(img, carry):
        rows = rows_at(img, IROWS)
        upstream = dot_nn(perm_ref[...], g_ref[first + img]) * live_ref[img]
        gb_ref[rows, :] = upstream.astype(BF16)
        small_ref[7:8, :] += jnp.sum(upstream, axis=0, keepdims=True)
        for part in range(hidden // FCHUNK):
            at = part * FCHUNK
            slope = slope_ref[rows, at : at + FCHUNK].astype(F32)
            dpre = dot_nt(gb_ref[rows, :], wdown_ref[at : at + FCHUNK, :]) * slope
            small_ref[8 + part : 9 + part, :] += jnp.sum(dpre, axis=0, keepdims=True)
            dpre_ref[rows, at : at + FCHUNK] = dpre.astype(BF16)
        dnorm = dot_nt(dpre_ref[rows, :], wup_ref[...])
        scaled, inv_std = normalize(res_ref[rows, :])
        small_ref[5:6, :] += jnp.sum(dnorm * scaled, axis=0, keepdims=True)
        small_ref[6:7, :] += jnp.sum(dnorm, axis=0, keepdims=True)
        dres = gb_ref[rows, :].astype(F32) + norm_back(dnorm, scaled, inv_std, vec_ref[5:6, :])
        dres_ref[rows, :] = dres
        small_ref[4:5, :] += jnp.sum(dres, axis=0, keepdims=True)
        dresb_ref[rows, :] = dres.astype(BF16)
        dmix_ref[rows, :] = dot_nt(dresb_ref[rows, :], wout_ref[...]).astype(BF16)
        return carry

    lax.fori_loop(0, images, step, 0)
    span = hidden // 2
    for side, dest in ((0, keep_ref), (1, send_ref)):
        half = section if side == 0 else 1 - section

        def down(part, carry, half=half, dest=dest):
            cols = pl.ds(pl.multiple_of(half * span + part * FCHUNK, FCHUNK), FCHUNK)
            dest[rows_at(part, FCHUNK), :] = dot_tn(act_ref[:, cols], gb_ref[...]).astype(BF16)
            return carry

        lax.fori_loop(0, span // FCHUNK, down, 0, unroll=True)
        cols = rows_at(half, width // 2)

        def up(part, carry, cols=cols, dest=dest):
            block = dot_tn(n2_ref[:, cols], dpre_ref[:, rows_at(part, width)])
            place = pl.ds(pl.multiple_of(span + part * (width // 2), width // 2), width // 2)
            dest[place, :] = block.astype(BF16)
            return carry

        lax.fori_loop(0, hidden // width, up, 0, unroll=True)
        dest[2 * span :, :] = dot_tn(mix_ref[:, cols], dresb_ref[...]).astype(BF16)


def attn_back_kernel(
    base_ref, perm_ref, vec_ref, wqkv_ref, xa_ref, nrm_ref, qkv_ref, prob_ref, dres_ref, dmix_ref,
    igrad_ref, igrad_b_ref, keep_ref, send_ref, tiles_ref, small_ref, dqkv_ref,
    *, images, head_dim,
):
    width = wqkv_ref.shape[0]
    groups = width // LANES
    factor = head_dim ** (-0.5)
    section = base_ref[1]
    small_ref[...] = jnp.zeros_like(small_ref)
    tiles_ref[...] = jnp.zeros_like(tiles_ref)
    mask = head_mask(head_dim)

    def attend(win, carry):
        rows = rows_at(win, PADW)
        for grp in range(groups):
            at = grp * LANES
            query = qkv_ref[rows, at : at + LANES]
            key = qkv_ref[rows, width + at : width + at + LANES]
            value = qkv_ref[rows, 2 * width + at : 2 * width + at + LANES]
            dmix = expand(dmix_ref[rows, at : at + LANES], mask)
            prob = prob_ref[win, grp]
            dprob = dot_nt(value, dmix)
            dvalue = dot_nn(prob.astype(BF16), dmix)
            dscore = prob * (dprob - jnp.sum(prob * dprob, axis=0, keepdims=True))
            tiles_ref[grp] += dscore
            dscore_b = dscore.astype(BF16)
            dkey = dot_nn(dscore_b, expand(query, mask))
            dquery = collapse(dot_tn(dscore_b, key), head_dim) * factor
            small_ref[2:3, at : at + LANES] += jnp.sum(dquery, axis=0, keepdims=True)
            small_ref[3:4, at : at + LANES] += jnp.sum(dvalue, axis=0, keepdims=True)
            dqkv_ref[rows, at : at + LANES] = dquery.astype(BF16)
            dqkv_ref[rows, width + at : width + at + LANES] = dkey.astype(BF16)
            dqkv_ref[rows, 2 * width + at : 2 * width + at + LANES] = dvalue.astype(BF16)
        return carry

    lax.fori_loop(0, images * NWIN, attend, 0)

    def leave(img, carry):
        rows = rows_at(img, IROWS)
        dnorm = dot_nt(dqkv_ref[rows, :], wqkv_ref[...])
        scaled, inv_std = normalize(xa_ref[rows, :].astype(F32))
        small_ref[0:1, :] += jnp.sum(dnorm * scaled, axis=0, keepdims=True)
        small_ref[1:2, :] += jnp.sum(dnorm, axis=0, keepdims=True)
        grad = dres_ref[rows, :] + norm_back(dnorm, scaled, inv_std, vec_ref[0:1, :])
        high = grad.astype(BF16)
        low = (grad - high.astype(F32)).astype(BF16)
        moved = dot_tn(perm_ref[...], high)
        igrad_b_ref[img] = moved.astype(BF16)
        igrad_ref[img] = moved + dot_tn(perm_ref[...], low)
        return carry

    lax.fori_loop(0, images, leave, 0)
    for side, dest in ((0, keep_ref), (1, send_ref)):
        half = section if side == 0 else 1 - section
        cols = rows_at(half, width // 2)

        def part_grad(part, carry, cols=cols, dest=dest):
            block = dot_tn(nrm_ref[:, cols], dqkv_ref[:, rows_at(part, width)])
            dest[rows_at(part, width // 2), :] = block.astype(BF16)
            return carry

        lax.fori_loop(0, 3, part_grad, 0, unroll=True)


def vmem():
    return pl.BlockSpec(memory_space=pltpu.VMEM)


def smem():
    return pl.BlockSpec(memory_space=pltpu.SMEM)


def shape_of(shape, dtype):
    return jax.ShapeDtypeStruct(shape, dtype)


PARAMS = pltpu.CompilerParams(vmem_limit_bytes=16 * 1024 * 1024)
SPILL_PARAMS = pltpu.CompilerParams(vmem_limit_bytes=30 * 1024 * 1024)
SMALL_PARAMS = pltpu.CompilerParams(vmem_limit_bytes=16 * 1024 * 1024)


def busy(micros):
    return pl.CostEstimate(flops=micros * 1000000000, transcendentals=0, bytes_accessed=1000000)


def run_forward(base, rows_in, perm, bias, vec, weights, images, head_dim, masked):
    wqkv, wout, wup, wdown = weights
    width, hidden = wup.shape
    total = images * IROWS
    shapes = (
        shape_of((images, SIDE * SIDE, width), BF16),
        shape_of((total, width), BF16),
        shape_of((total, width), BF16),
        shape_of((total, 3 * width), BF16),
        shape_of((images * NWIN, width // LANES, PADW, GROUP * PADW), F32),
        shape_of((total, width), BF16),
        shape_of((total, width), F32),
        shape_of((total, width), BF16),
        shape_of((total, hidden), BF16),
        shape_of((total, hidden), BF16),
    )
    spill = not masked
    scratch = []
    if spill:
        scratch = [pltpu.VMEM(shape.shape, shape.dtype) for shape in shapes[1:]]
        scratch += [pltpu.SemaphoreType.DMA((5,)), pltpu.SemaphoreType.DMA((9, images))]
    return pl.pallas_call(
        functools.partial(forward_kernel, images=images, head_dim=head_dim, masked=masked, spill=spill),
        out_shape=shapes,
        in_specs=[smem()] + [vmem()] * 8,
        out_specs=(vmem(), *(pl.BlockSpec(memory_space=pl.ANY) if spill else vmem() for _ in shapes[1:])),
        scratch_shapes=scratch,
        compiler_params=SPILL_PARAMS if spill else PARAMS,
        cost_estimate=busy(13),
        name="layer_forward",
    )(base, rows_in, perm, bias, vec, wqkv, wout, wup, wdown)


def run_ffn_back(base, g_rows, live, perm, vec, weights, kept, images):
    _, wout, wup, wdown = weights
    _, _, _, _, mix, res, n2, act, slope = kept
    width, hidden = wup.shape
    total = images * IROWS
    shapes = (
        shape_of((total, width), F32),
        shape_of((total, width), BF16),
        shape_of((hidden + width // 2, width), BF16),
        shape_of((hidden + width // 2, width), BF16),
        shape_of((SMALL_ROWS, width), F32),
    )
    return pl.pallas_call(
        functools.partial(ffn_back_kernel, images=images),
        out_shape=shapes,
        in_specs=[smem(), vmem(), smem()] + [vmem()] * 10,
        out_specs=tuple(vmem() for _ in shapes),
        scratch_shapes=[
            pltpu.VMEM((total, width), BF16),
            pltpu.VMEM((total, hidden), BF16),
            pltpu.VMEM((total, width), BF16),
        ],
        compiler_params=PARAMS,
        cost_estimate=busy(9),
        name="ffn_back",
    )(base, g_rows, live, perm, vec, wout, wup, wdown, mix, res, n2, act, slope)


def run_attn_back(base, perm, vec, weights, kept, dres, dmix, images, head_dim):
    wqkv = weights[0]
    xa, nrm, qkv, prob = kept[:4]
    width = wqkv.shape[0]
    total = images * IROWS
    shapes = (
        shape_of((images, SIDE * SIDE, width), F32),
        shape_of((images, SIDE * SIDE, width), BF16),
        shape_of((3 * width // 2, width), BF16),
        shape_of((3 * width // 2, width), BF16),
        shape_of((width // LANES, PADW, GROUP * PADW), F32),
        shape_of((SMALL_ROWS, width), F32),
    )
    return pl.pallas_call(
        functools.partial(attn_back_kernel, images=images, head_dim=head_dim),
        out_shape=shapes,
        in_specs=[smem()] + [vmem()] * 9,
        out_specs=tuple(vmem() for _ in shapes),
        scratch_shapes=[pltpu.VMEM((total, 3 * width), BF16)],
        compiler_params=PARAMS,
        cost_estimate=busy(13),
        name="attn_back",
    )(base, perm, vec, wqkv, xa, nrm, qkv, prob, dres, dmix)


def round_orders(bits):
    if bits == 4:
        return ((0, 1, 2, 3), (1, 0, 3, 2), (2, 3, 0, 1), (3, 2, 0, 1))
    axes = list(range(bits))
    return tuple(tuple(axes[turn:] + axes[:turn]) for turn in range(4))


def added(left, right):
    return (left.astype(F32) + right.astype(F32)).astype(BF16)


def first_ffn_kernel(bit_ref, keep_ref, recv_ref, *outs, turn):
    tail_ref = outs[4]
    for color in range(2):
        half = outs[color].shape[0]
        bit = bit_ref[turn + color]
        for side, place in ((0, bit), (2, 1 - bit)):
            rows = pl.ds(pl.multiple_of(color * 2 * half + place * half, half), half)
            outs[side + color][...] = added(keep_ref[rows, :], recv_ref[rows, :])
    tail = keep_ref.shape[0] - tail_ref.shape[0]
    tail_ref[...] = added(keep_ref[tail:, :], recv_ref[tail:, :])


def first_qkv_kernel(bit_ref, tail_ref, keep_ref, recv_ref, *outs, turn):
    half = outs[0].shape[0]
    head = added(keep_ref[:half, :], recv_ref[:half, :])
    low = bit_ref[turn + 2] == 0
    outs[0][...] = jnp.where(low, tail_ref[...], head)
    outs[2][...] = jnp.where(low, head, tail_ref[...])
    bit = bit_ref[turn + 3]
    for side, place in ((1, bit), (3, 1 - bit)):
        rows = pl.ds(pl.multiple_of(half + place * half, half), half)
        outs[side][...] = added(keep_ref[rows, :], recv_ref[rows, :])


def sum_kernel(bit_ref, *refs, turn):
    keep, recv, outs = refs[:4], refs[4:8], refs[8:]
    for color in range(4):
        half = keep[color].shape[0] // 2
        bit = bit_ref[turn + color]
        for side, start in ((0, bit * half), (4, (1 - bit) * half)):
            rows = pl.ds(pl.multiple_of(start, 8), half)
            outs[side + color][...] = added(keep[color][rows, :], recv[color][rows, :])


def last_kernel(bit_ref, *refs, turn):
    keep, recv, out_ref = refs[:4], refs[4:8], refs[8]
    at = 0
    for color in range(4):
        size = keep[color].shape[0]
        out_ref[at : at + size, :] = added(keep[color][...], recv[color][...])
        at += size


def split_small(value):
    high = value.astype(BF16)
    return high, (value - high.astype(F32)).astype(BF16)


def pick_kernel(section_ref, zero_ref, one_ref, small_zero_ref, small_one_ref, own_ref, send_ref, *, turn):
    first = section_ref[0] == 0
    size = zero_ref.shape[0]
    own_ref[:size, :] = jnp.where(first, zero_ref[...], one_ref[...])
    send_ref[:size, :] = jnp.where(first, one_ref[...], zero_ref[...])
    for dest, value in (
        (own_ref, jnp.where(first, small_zero_ref[...], small_one_ref[...])),
        (send_ref, jnp.where(first, small_one_ref[...], small_zero_ref[...])),
    ):
        high, low = split_small(value)
        dest[size : size + EXTRA, :] = high
        dest[size + EXTRA :, :] = low


def join_kernel(section_ref, own_ref, got_ref, *outs, turn):
    first = section_ref[0] == 0
    at = 0
    for color in range(4):
        size = outs[color].shape[1] - (EXTRA if color == 3 else 0)
        mine, other = own_ref[at : at + size, :], got_ref[at : at + size, :]
        outs[color][0, :size, :] = jnp.where(first, mine, other)
        outs[color][1, :size, :] = jnp.where(first, other, mine)
        at += size
    total = jnp.zeros((EXTRA, own_ref.shape[1]), F32)
    for ref in (own_ref, got_ref):
        total += ref[at : at + EXTRA, :].astype(F32) + ref[at + EXTRA :, :].astype(F32)
    high, low = split_small(total)
    outs[3][0, size:, :] = high
    outs[3][1, size:, :] = low


def small_total(own_ref, recv_ref):
    total = jnp.zeros((EXTRA, own_ref.shape[2]), F32)
    at = own_ref.shape[1] - EXTRA
    for ref in (own_ref, recv_ref):
        total += ref[0, at:, :].astype(F32) + ref[1, at:, :].astype(F32)
    return total


def merge_kernel(bit_ref, *refs, turn):
    own, recv, outs = refs[:4], refs[4:8], refs[8:]
    for color in range(4):
        size = own[color].shape[1] - (EXTRA if color == 3 else 0)
        bit = bit_ref[turn + color]
        outs[color][:, pl.ds(pl.multiple_of(bit * size, 8), size), :] = own[color][:, :size, :]
        outs[color][:, pl.ds(pl.multiple_of((1 - bit) * size, 8), size), :] = recv[color][:, :size, :]
    high, low = split_small(small_total(own[3], recv[3]))
    outs[3][0, 2 * size :, :] = high
    outs[3][1, 2 * size :, :] = low


def final_kernel(bit_ref, *refs, turn):
    own, recv = refs[:4], refs[4:8]
    down_ref, up_ref, out_ref, qkv_ref = refs[8:12]
    rows_refs, up_bias_ref, table_ref = refs[12:20], refs[20], refs[21]
    width = out_ref.shape[1]
    part = width // 2
    for half in range(2):
        rows = slice(half * part, (half + 1) * part)
        bit = bit_ref[turn + 0]
        span = own[0].shape[1]
        for side, source in ((bit, own[0]), (1 - bit, recv[0])):
            down_ref[pl.ds(pl.multiple_of(half * 2 * span + side * span, span), span), :] = source[half].astype(F32)
        bit = bit_ref[turn + 1]
        blocks = own[1].shape[1] // part
        for side, source in ((bit, own[1]), (1 - bit, recv[1])):
            for block in range(blocks):
                cols = pl.ds(pl.multiple_of((side * blocks + block) * width, width), width)
                up_ref[rows, cols] = source[half, block * part : (block + 1) * part, :].astype(F32)
        is_low = bit_ref[turn + 2] == 0
        mine, other = own[2][half].astype(F32), recv[2][half].astype(F32)
        out_ref[rows, :] = jnp.where(is_low, mine, other)
        qkv_ref[rows, :width] = jnp.where(is_low, other, mine)
        bit = bit_ref[turn + 3]
        size = own[3].shape[1] - EXTRA
        for side, source in ((bit, own[3]), (1 - bit, recv[3])):
            cols = pl.ds(pl.multiple_of((1 + side) * width, width), width)
            qkv_ref[rows, cols] = source[half, :size, :].astype(F32)
    total = small_total(own[3], recv[3])
    for number, ref in enumerate(rows_refs):
        ref[...] = total[number : number + 1, :]
    for block in range(up_bias_ref.shape[1] // width):
        up_bias_ref[:, block * width : (block + 1) * width] = total[8 + block : 9 + block, :]
    table_ref[...] = total[SMALL_ROWS:, : table_ref.shape[1]]


def small_call(kernel, bits, arrays, shapes, turn=0):
    return pl.pallas_call(
        functools.partial(kernel, turn=4 * turn),
        out_shape=tuple(shapes),
        in_specs=[smem()] + [vmem()] * len(arrays),
        out_specs=tuple(vmem() for _ in shapes),
        compiler_params=SMALL_PARAMS,
    )(bits, *arrays)


def exchange(value, bit, count):
    return lax.ppermute(value, "dp", [(one, one ^ (1 << bit)) for one in range(count)])


def start_rounds(keep_ffn, send_ffn, keep_qkv, send_qkv, place_bits):
    width = keep_ffn.shape[1]
    recv_ffn = swap(send_ffn)
    recv_qkv = swap(send_qkv)
    long = shape_of(((keep_ffn.shape[0] - width // 2) // 4, width), BF16)
    short = shape_of((width // 2, width), BF16)
    *ffn, tail = small_call(first_ffn_kernel, place_bits, (keep_ffn, recv_ffn), [long] * 4 + [short])
    rest = small_call(first_qkv_kernel, place_bits, (tail, keep_qkv, recv_qkv), [short] * 4)
    return (*ffn[:2], *rest[:2], *ffn[2:], *rest[2:])


def reduce_rounds(parts, orders, place_bits, count):
    width = parts[0].shape[1]
    rounds = len(orders[0])
    for turn in range(rounds):
        mine, gone = parts[:4], parts[4:]
        recv = [exchange(part, order[turn], count) for part, order in zip(gone, orders)]
        if turn + 1 < rounds:
            halves = [shape_of((part.shape[0] // 2, width), BF16) for part in mine]
            parts = small_call(sum_kernel, place_bits, list(mine) + recv, halves * 2, turn + 1)
        else:
            total = shape_of((sum(part.shape[0] for part in mine), width), BF16)
            parts = small_call(last_kernel, place_bits, list(mine) + recv, [total])
    return parts[0]


def gather_layer(shard_zero, shard_one, small_zero, small_one, where, sizes, hidden, entries, heads, orders, place_bits, count):
    rows, width = shard_zero.shape
    both_shape = [shape_of((rows + 2 * EXTRA, width), BF16)] * 2
    own, send = small_call(pick_kernel, where, (shard_zero, shard_one, small_zero, small_one), both_shape)
    got = swap(send)
    extras = (0, 0, 0, EXTRA)
    shapes = [shape_of((2, size + extra, width), BF16) for size, extra in zip(sizes, extras)]
    parts = small_call(join_kernel, where, (own, got), shapes)
    rounds = len(orders[0])
    for turn in reversed(range(rounds)):
        recv = [exchange(part, order[turn], count) for part, order in zip(parts, orders)]
        if turn:
            shapes = [
                shape_of((2, 2 * part.shape[1] - extra, width), BF16) for part, extra in zip(parts, extras)
            ]
            parts = small_call(merge_kernel, place_bits, list(parts) + recv, shapes, turn)
    shapes = [shape_of((hidden, width), F32), shape_of((width, hidden), F32), shape_of((width, width), F32),
              shape_of((width, 3 * width), F32)]
    shapes += [shape_of((1, width), F32)] * 8 + [shape_of((1, hidden), F32), shape_of((heads, entries), F32)]
    return small_call(final_kernel, place_bits, list(parts) + recv, shapes)


def swap(value):
    return lax.ppermute(value, "section", [(0, 1), (1, 0)])


def both(value, section):
    other = swap(value)
    first = jnp.where(section == 0, value, other)
    second = jnp.where(section == 0, other, value)
    return first, second


def body(
    images,
    cotangent,
    image_count,
    norm1_gain,
    norm1_bias,
    qkv_weight,
    query_bias,
    value_bias,
    bias_table,
    out_weight,
    out_bias,
    norm2_gain,
    norm2_bias,
    up_weight,
    up_bias,
    down_weight,
    down_bias,
):
    section = lax.axis_index("section")
    slots = images.shape[0]
    mine = slots // 2
    width = images.shape[-1]
    heads = bias_table.shape[-1]
    head_dim = width // heads
    vectors = jnp.concatenate(
        [norm1_gain, norm1_bias, query_bias, value_bias, out_bias, norm2_gain, norm2_bias, down_bias,
         up_bias.reshape(-1, width)], axis=0)
    layer_vec = both(vectors, section)
    layer_table = both(bias_table[0], section)
    layer_w = list(zip(*[both(weight[0], section) for weight in (qkv_weight, out_weight, up_weight, down_weight)]))
    perms = [jnp.asarray(window_onehot(shift), BF16) for shift in (0, SHIFT)]
    onehot = pair_onehot()
    biases = bias_tiles(jnp.stack(layer_table), onehot)
    base_mine = jnp.stack([section * mine, section]).astype(jnp.int32)
    base_zero = jnp.stack([section * 0, section]).astype(jnp.int32)
    live = (section * mine + jnp.arange(mine) < image_count[0]).astype(F32)
    ones = jnp.ones((mine,), F32)
    count = lax.axis_size("dp")
    bits = count.bit_length() - 1
    chip = lax.axis_index("dp")
    orders = round_orders(bits)
    turns = np.array([[order[turn] for order in orders] for turn in range(bits)]).reshape(-1)
    place_bits = (chip >> turns.astype(np.int32)) & 1

    out_zero, *kept_zero = run_forward(base_mine, images, perms[0], biases[0], layer_vec[0], layer_w[0], mine, head_dim, False)
    out_one, *kept_one = run_forward(base_zero, out_zero, perms[1], biases[1], layer_vec[1], layer_w[1], mine, head_dim, True)

    def backward(layer, base, g_rows, alive, kept):
        dres, dmix, keep_ffn, send_ffn, small_ffn = run_ffn_back(
            base, g_rows, alive, perms[layer], layer_vec[layer], layer_w[layer], kept, mine)
        igrad, igrad_b, keep_qkv, send_qkv, tiles, small_attn = run_attn_back(
            base, perms[layer], layer_vec[layer], layer_w[layer], kept, dres, dmix, mine, head_dim)
        parts = start_rounds(keep_ffn, send_ffn, keep_qkv, send_qkv, place_bits)
        shard = reduce_rounds(parts, orders, place_bits, count)
        return igrad, igrad_b, shard, (tiles, small_ffn + small_attn), parts

    igrad_one, back_rows, shard_one, rest_one, parts = backward(1, base_mine, cotangent, live, kept_one)
    halves = [part.shape[0] for part in parts[:4]]
    igrad_zero, _, shard_zero, rest_zero, parts = backward(0, base_zero, back_rows, ones, kept_zero)

    def finish_small(rest):
        (tiles, vecs), _ = lax.optimization_barrier((rest, parts[2]))
        table = table_grad(tiles, heads, onehot)
        return jnp.concatenate([vecs, jnp.pad(table, ((0, 0), (0, width - table.shape[1])))])

    small_zero, small_one = finish_small(rest_zero), finish_small(rest_one)

    hidden = up_bias.shape[1]
    sizes = [half >> (bits - 1) for half in halves]
    where = section.astype(jnp.int32).reshape(1)
    g_down, g_up, g_out, g_qkv, *vecs, g_up_b, g_table = gather_layer(
        shard_zero, shard_one, small_zero, small_one, where, sizes, hidden, bias_table.shape[1], heads, orders,
        place_bits, count)

    def place(first, second):
        got = swap(jnp.where(section == 0, second, first))
        upper = jnp.concatenate([first, got], axis=0)
        lower = jnp.concatenate([got, second], axis=0)
        return jnp.where(section == 0, upper, lower)

    segment_out = place(out_zero, out_one)
    input_grad = place(igrad_zero, igrad_one)
    g_gain_one, g_bias_one, g_query, g_value, g_out_b, g_gain_two, g_bias_two, g_down_b = vecs
    return (
        segment_out[None], input_grad[None], g_gain_one, g_bias_one, g_qkv[None], g_query, g_value, g_table.T[None],
        g_out[None], g_out_b, g_gain_two, g_bias_two, g_up[None], g_up_b, g_down[None], g_down_b,
    )


def solution(mesh):
    row = P("section", None)
    mat = P("section", None, None)

    return jax.shard_map(
        body,
        mesh=mesh,
        in_specs=(
            P("dp", None, None), P("dp", None, None), P("dp"),
            row, row, mat, row, row, mat, mat, row, row, row, mat, row, mat, row,
        ),
        out_specs=(
            P("section", "dp", None, None), P("section", "dp", None, None),
            row, row, mat, row, row, mat, mat, row, row, row, mat, row, mat, row,
        ),
        check_vma=False,
    )
```

```python
import functools

import jax
import jax.numpy as jnp
import numpy as np
from jax import lax
from jax.experimental import pallas as pl
from jax.experimental.pallas import tpu as pltpu
from jax.sharding import PartitionSpec as P


WIN = 7
SIDE = 14
SHIFT = 3
CELLS = WIN * WIN
PADW = 64
NWIN = (SIDE // WIN) ** 2
IROWS = NWIN * PADW
GROUP = 4
LANES = 128
FCHUNK = 512
EPS = 1e-05
MASKED = -100.0
PADDED = -1e30
SQRT_HALF = 0.7071067811865476
INV_ROOT_TAU = 0.3989422804014327
F32 = jnp.float32
BF16 = jnp.bfloat16
SMALL_ROWS = 16
EXTRA = 32


def window_source(offset):
    across = SIDE // WIN
    places = np.arange(SIDE * SIDE)
    window_no = places // CELLS
    cell_no = places % CELLS
    grid_row = window_no // across * WIN + cell_no // WIN
    grid_col = window_no % across * WIN + cell_no % WIN
    source = (grid_row + offset) % SIDE * SIDE + (grid_col + offset) % SIDE
    return window_no * PADW + cell_no, source


def window_onehot(offset):
    rows, source = window_source(offset)
    table = np.zeros((IROWS, SIDE * SIDE), np.float32)
    table[rows, source] = 1.0
    return table


def region_mask():
    places = np.arange(SIDE)
    labels = (places >= SIDE - WIN).astype(np.int32) + (places >= SIDE - SHIFT).astype(np.int32)
    region = (labels[:, None] * 3 + labels[None, :]).reshape(-1)
    rows, source = window_source(0)
    padded = np.full((IROWS,), -1)
    padded[rows] = region[source]
    padded = padded.reshape(NWIN, PADW)
    differ = (padded[:, :, None] != padded[:, None, :]) & (padded[:, :, None] >= 0)
    differ &= padded[:, None, :] >= 0
    return np.where(differ, MASKED, 0.0).astype(np.float32)


def relative_index():
    cells = np.arange(CELLS)
    row_of, col_of = cells // WIN, cells % WIN
    row_gap = row_of[:, None] - row_of[None, :] + WIN - 1
    return row_gap * (2 * WIN - 1) + col_of[:, None] - col_of[None, :] + WIN - 1


def pair_onehot():
    index = np.full((PADW, PADW), -1, np.int32)
    index[:CELLS, :CELLS] = relative_index().T
    entries = lax.broadcasted_iota(jnp.int32, ((2 * WIN - 1) ** 2, PADW * PADW), 0)
    return (entries == jnp.asarray(index.reshape(1, -1))).astype(BF16)


def three_terms(value):
    high = lax.reduce_precision(value, 8, 7)
    mid = lax.reduce_precision(value - high, 8, 7)
    return jnp.stack([high, mid, value - high - mid]).astype(BF16)


def bias_tiles(tables, onehot):
    layers, _, heads = tables.shape
    terms = three_terms(tables.transpose(0, 2, 1)).reshape(3 * layers * heads, -1)
    spread = dot_nn(terms, onehot).reshape(3, layers * heads, -1).sum(axis=0)
    tiles = spread.reshape(layers, heads // GROUP, GROUP, PADW, PADW).transpose(0, 1, 3, 2, 4)
    pad_key = np.where(np.arange(PADW) >= CELLS, PADDED, 0.0).astype(np.float32)
    tiles = tiles + pad_key[None, None, :, None, None]
    plain = tiles[0][None]
    masked = tiles[1][None] + region_mask()[:, None, :, None, :]
    return [part.reshape(part.shape[0], heads // GROUP, PADW, GROUP * PADW) for part in (plain, masked)]


def table_grad(tiles, heads, onehot):
    spread = tiles.reshape(heads // GROUP, PADW, GROUP, PADW).transpose(0, 2, 1, 3)
    terms = three_terms(spread.reshape(heads, PADW * PADW)).reshape(3 * heads, -1)
    return dot_nt(terms, onehot).reshape(3, heads, -1).sum(axis=0)


def dot_nn(left, right):
    return lax.dot_general(left, right, (((1,), (0,)), ((), ())), preferred_element_type=F32)


def dot_nt(left, right):
    return lax.dot_general(left, right, (((1,), (1,)), ((), ())), preferred_element_type=F32)


def dot_tn(left, right):
    return lax.dot_general(left, right, (((0,), (0,)), ((), ())), preferred_element_type=F32)


def normalize(values):
    centered = values - jnp.mean(values, axis=-1, keepdims=True)
    inv_std = lax.rsqrt(jnp.mean(centered * centered, axis=-1, keepdims=True) + EPS)
    return centered * inv_std, inv_std


def norm_back(upstream, scaled, inv_std, gain):
    along = upstream * gain
    return inv_std * (
        along
        - jnp.mean(along, axis=-1, keepdims=True)
        - scaled * jnp.mean(along * scaled, axis=-1, keepdims=True)
    )


def gelu_parts(pre):
    cdf_val = 0.5 * (1.0 + lax.erf(pre * SQRT_HALF))
    density = jnp.exp(-0.5 * pre * pre) * INV_ROOT_TAU
    return pre * cdf_val, cdf_val + pre * density


def head_mask(head_dim):
    rows = lax.broadcasted_iota(jnp.int32, (GROUP * PADW, LANES), 0) // PADW
    cols = lax.broadcasted_iota(jnp.int32, (GROUP * PADW, LANES), 1) // head_dim
    return jnp.where(rows == cols, 1.0, 0.0).astype(BF16)


def expand(tile, mask):
    return jnp.concatenate([tile] * GROUP, axis=0) * mask


def collapse(wide, head_dim):
    head_of = lax.broadcasted_iota(jnp.int32, (PADW, LANES), 1) // head_dim
    total = wide[:PADW]
    for head in range(1, GROUP):
        total = jnp.where(head_of == head, wide[head * PADW : (head + 1) * PADW], total)
    return total


def rows_at(number, size):
    return pl.ds(pl.multiple_of(number * size, size), size)


def forward_kernel(
    base_ref, x_ref, perm_ref, bias_ref, vec_ref, wqkv_ref, wout_ref, wup_ref, wdown_ref,
    out_ref, *refs, images, head_dim, masked, spill,
):
    kept = refs[9:18] if spill else refs
    xa_ref, nrm_ref, qkv_ref, prob_ref, mix_ref, res_ref, n2_ref, act_ref, slope_ref = kept

    def whole_copy(number):
        return pltpu.make_async_copy(kept[number], refs[number], refs[18].at[number])

    def image_copy(number, img):
        rows = rows_at(img, IROWS)
        return pltpu.make_async_copy(kept[number].at[rows, :], refs[number].at[rows, :], refs[19].at[number, img])

    width = wout_ref.shape[0]
    hidden = wup_ref.shape[1]
    groups = width // LANES
    factor = head_dim ** (-0.5)
    first = base_ref[0]

    def enter(img, carry):
        rows = rows_at(img, IROWS)
        entry = dot_nn(perm_ref[...], x_ref[first + img])
        xa_ref[rows, :] = entry.astype(BF16)
        scaled, _ = normalize(entry)
        normed = (scaled * vec_ref[0:1, :] + vec_ref[1:2, :]).astype(BF16)
        nrm_ref[rows, :] = normed
        query = (dot_nn(normed, wqkv_ref[:, :width]) + vec_ref[2:3, :]) * factor
        qkv_ref[rows, :width] = query.astype(BF16)
        qkv_ref[rows, width : 2 * width] = dot_nn(normed, wqkv_ref[:, width : 2 * width]).astype(BF16)
        value = dot_nn(normed, wqkv_ref[:, 2 * width :]) + vec_ref[3:4, :]
        qkv_ref[rows, 2 * width :] = value.astype(BF16)
        return carry

    lax.fori_loop(0, images, enter, 0)
    if spill:
        for number in range(3):
            whole_copy(number).start()
    mask = head_mask(head_dim)

    def attend(win, carry):
        rows = rows_at(win, PADW)
        bias_no = win % NWIN if masked else 0
        for grp in range(groups):
            at = grp * LANES
            query = qkv_ref[rows, at : at + LANES]
            key = qkv_ref[rows, width + at : width + at + LANES]
            value = qkv_ref[rows, 2 * width + at : 2 * width + at + LANES]
            score = dot_nt(key, expand(query, mask)) + bias_ref[bias_no, grp]
            expo = jnp.exp(score - jnp.max(score, axis=0, keepdims=True))
            prob = expo * (1.0 / jnp.sum(expo, axis=0, keepdims=True))
            prob_ref[win, grp] = prob
            wide = dot_tn(prob.astype(BF16), value)
            mix_ref[rows, at : at + LANES] = collapse(wide, head_dim).astype(BF16)
        return carry

    lax.fori_loop(0, images * NWIN, attend, 0)
    if spill:
        for number in range(3, 5):
            whole_copy(number).start()

    def leave(img, carry):
        rows = rows_at(img, IROWS)
        entry = xa_ref[rows, :].astype(F32)
        resid = entry + dot_nn(mix_ref[rows, :], wout_ref[...]) + vec_ref[4:5, :]
        res_ref[rows, :] = resid
        scaled, _ = normalize(resid)
        n2_ref[rows, :] = (scaled * vec_ref[5:6, :] + vec_ref[6:7, :]).astype(BF16)
        for part in range(hidden // FCHUNK):
            at = part * FCHUNK
            pre = dot_nn(n2_ref[rows, :], wup_ref[:, at : at + FCHUNK]) + vec_ref[8 + part : 9 + part, :]
            activ, slope = gelu_parts(pre)
            act_ref[rows, at : at + FCHUNK] = activ.astype(BF16)
            slope_ref[rows, at : at + FCHUNK] = slope.astype(BF16)
        done = res_ref[rows, :] + dot_nn(act_ref[rows, :], wdown_ref[...]) + vec_ref[7:8, :]
        out_ref[img] = dot_tn(perm_ref[...], done.astype(BF16)).astype(BF16)
        if spill:
            for number in range(5, 9):
                image_copy(number, img).start()
        return carry

    lax.fori_loop(0, images, leave, 0)
    if spill:
        for number in range(5):
            whole_copy(number).wait()
        for img in range(images):
            for number in range(5, 9):
                image_copy(number, img).wait()


def ffn_back_kernel(
    base_ref, g_ref, live_ref, perm_ref, vec_ref, wout_ref, wup_ref, wdown_ref,
    mix_ref, res_ref, n2_ref, act_ref, slope_ref,
    dres_ref, dmix_ref, keep_ref, send_ref,
    small_ref, gb_ref, dpre_ref, dresb_ref, *local,
    images,
):
    fetches = ()
    if local:
        *local, sem = local
        sources = (mix_ref, res_ref, n2_ref, act_ref, slope_ref)
        fetches = [
            pltpu.make_async_copy(source, dest, sem.at[number])
            for number, (source, dest) in enumerate(zip(sources, local))
        ]
        for fetch in reversed(fetches):
            fetch.start()
        mix_ref, res_ref, n2_ref, act_ref, slope_ref = local
    width = wout_ref.shape[0]
    hidden = wup_ref.shape[1]
    first = base_ref[0]
    section = base_ref[1]
    small_ref[...] = jnp.zeros_like(small_ref)
    if fetches:
        fetches[4].wait()
        fetches[1].wait()

    def step(img, carry):
        rows = rows_at(img, IROWS)
        upstream = dot_nn(perm_ref[...], g_ref[first + img]) * live_ref[img]
        gb_ref[rows, :] = upstream.astype(BF16)
        small_ref[7:8, :] += jnp.sum(upstream, axis=0, keepdims=True)
        for part in range(hidden // FCHUNK):
            at = part * FCHUNK
            slope = slope_ref[rows, at : at + FCHUNK].astype(F32)
            dpre = dot_nt(gb_ref[rows, :], wdown_ref[at : at + FCHUNK, :]) * slope
            small_ref[8 + part : 9 + part, :] += jnp.sum(dpre, axis=0, keepdims=True)
            dpre_ref[rows, at : at + FCHUNK] = dpre.astype(BF16)
        dnorm = dot_nt(dpre_ref[rows, :], wup_ref[...])
        scaled, inv_std = normalize(res_ref[rows, :])
        small_ref[5:6, :] += jnp.sum(dnorm * scaled, axis=0, keepdims=True)
        small_ref[6:7, :] += jnp.sum(dnorm, axis=0, keepdims=True)
        dres = gb_ref[rows, :].astype(F32) + norm_back(dnorm, scaled, inv_std, vec_ref[5:6, :])
        dres_ref[rows, :] = dres
        small_ref[4:5, :] += jnp.sum(dres, axis=0, keepdims=True)
        dresb_ref[rows, :] = dres.astype(BF16)
        dmix_ref[rows, :] = dot_nt(dresb_ref[rows, :], wout_ref[...]).astype(BF16)
        return carry

    lax.fori_loop(0, images, step, 0)
    span = hidden // 2
    for fetch in (fetches[0], fetches[2], fetches[3]) if fetches else ():
        fetch.wait()
    for side, dest in ((0, keep_ref), (1, send_ref)):
        half = section if side == 0 else 1 - section

        def down(part, carry, half=half, dest=dest):
            cols = pl.ds(pl.multiple_of(half * span + part * FCHUNK, FCHUNK), FCHUNK)
            dest[rows_at(part, FCHUNK), :] = dot_tn(act_ref[:, cols], gb_ref[...]).astype(BF16)
            return carry

        lax.fori_loop(0, span // FCHUNK, down, 0, unroll=True)
        cols = rows_at(half, width // 2)

        def up(part, carry, cols=cols, dest=dest):
            block = dot_tn(n2_ref[:, cols], dpre_ref[:, rows_at(part, width)])
            place = pl.ds(pl.multiple_of(span + part * (width // 2), width // 2), width // 2)
            dest[place, :] = block.astype(BF16)
            return carry

        lax.fori_loop(0, hidden // width, up, 0, unroll=True)
        dest[2 * span :, :] = dot_tn(mix_ref[:, cols], dresb_ref[...]).astype(BF16)


def attn_back_kernel(
    base_ref, perm_ref, vec_ref, wqkv_ref, xa_ref, nrm_ref, qkv_ref, prob_ref, dres_ref, dmix_ref,
    igrad_ref, igrad_b_ref, keep_ref, send_ref, tiles_ref, small_ref, dqkv_ref,
    *, images, head_dim,
):
    width = wqkv_ref.shape[0]
    groups = width // LANES
    factor = head_dim ** (-0.5)
    section = base_ref[1]
    small_ref[...] = jnp.zeros_like(small_ref)
    tiles_ref[...] = jnp.zeros_like(tiles_ref)
    mask = head_mask(head_dim)

    def attend(win, carry):
        rows = rows_at(win, PADW)
        for grp in range(groups):
            at = grp * LANES
            query = qkv_ref[rows, at : at + LANES]
            key = qkv_ref[rows, width + at : width + at + LANES]
            value = qkv_ref[rows, 2 * width + at : 2 * width + at + LANES]
            dmix = expand(dmix_ref[rows, at : at + LANES], mask)
            prob = prob_ref[win, grp]
            dprob = dot_nt(value, dmix)
            dvalue = dot_nn(prob.astype(BF16), dmix)
            dscore = prob * (dprob - jnp.sum(prob * dprob, axis=0, keepdims=True))
            tiles_ref[grp] += dscore
            dscore_b = dscore.astype(BF16)
            dkey = dot_nn(dscore_b, expand(query, mask))
            dquery = collapse(dot_tn(dscore_b, key), head_dim) * factor
            small_ref[2:3, at : at + LANES] += jnp.sum(dquery, axis=0, keepdims=True)
            small_ref[3:4, at : at + LANES] += jnp.sum(dvalue, axis=0, keepdims=True)
            dqkv_ref[rows, at : at + LANES] = dquery.astype(BF16)
            dqkv_ref[rows, width + at : width + at + LANES] = dkey.astype(BF16)
            dqkv_ref[rows, 2 * width + at : 2 * width + at + LANES] = dvalue.astype(BF16)
        return carry

    lax.fori_loop(0, images * NWIN, attend, 0)

    def leave(img, carry):
        rows = rows_at(img, IROWS)
        dnorm = dot_nt(dqkv_ref[rows, :], wqkv_ref[...])
        scaled, inv_std = normalize(xa_ref[rows, :].astype(F32))
        small_ref[0:1, :] += jnp.sum(dnorm * scaled, axis=0, keepdims=True)
        small_ref[1:2, :] += jnp.sum(dnorm, axis=0, keepdims=True)
        grad = dres_ref[rows, :] + norm_back(dnorm, scaled, inv_std, vec_ref[0:1, :])
        high = grad.astype(BF16)
        low = (grad - high.astype(F32)).astype(BF16)
        moved = dot_tn(perm_ref[...], high)
        igrad_b_ref[img] = moved.astype(BF16)
        igrad_ref[img] = moved + dot_tn(perm_ref[...], low)
        return carry

    lax.fori_loop(0, images, leave, 0)
    for side, dest in ((0, keep_ref), (1, send_ref)):
        half = section if side == 0 else 1 - section
        cols = rows_at(half, width // 2)

        def part_grad(part, carry, cols=cols, dest=dest):
            block = dot_tn(nrm_ref[:, cols], dqkv_ref[:, rows_at(part, width)])
            dest[rows_at(part, width // 2), :] = block.astype(BF16)
            return carry

        lax.fori_loop(0, 3, part_grad, 0, unroll=True)


def vmem():
    return pl.BlockSpec(memory_space=pltpu.VMEM)


def hbm():
    return pl.BlockSpec(memory_space=pltpu.HBM)


def smem():
    return pl.BlockSpec(memory_space=pltpu.SMEM)


def shape_of(shape, dtype):
    return jax.ShapeDtypeStruct(shape, dtype)


PARAMS = pltpu.CompilerParams(vmem_limit_bytes=16 * 1024 * 1024)
SPILL_PARAMS = pltpu.CompilerParams(vmem_limit_bytes=30 * 1024 * 1024)
SMALL_PARAMS = pltpu.CompilerParams(vmem_limit_bytes=16 * 1024 * 1024)


def busy(micros):
    return pl.CostEstimate(flops=micros * 1000000000, transcendentals=0, bytes_accessed=1000000)


def run_forward(base, rows_in, perm, bias, vec, weights, images, head_dim, masked):
    wqkv, wout, wup, wdown = weights
    width, hidden = wup.shape
    total = images * IROWS
    shapes = (
        shape_of((images, SIDE * SIDE, width), BF16),
        shape_of((total, width), BF16),
        shape_of((total, width), BF16),
        shape_of((total, 3 * width), BF16),
        shape_of((images * NWIN, width // LANES, PADW, GROUP * PADW), F32),
        shape_of((total, width), BF16),
        shape_of((total, width), F32),
        shape_of((total, width), BF16),
        shape_of((total, hidden), BF16),
        shape_of((total, hidden), BF16),
    )
    spill = not masked
    scratch = []
    if spill:
        scratch = [pltpu.VMEM(shape.shape, shape.dtype) for shape in shapes[1:]]
        scratch += [pltpu.SemaphoreType.DMA((5,)), pltpu.SemaphoreType.DMA((9, images))]
    return pl.pallas_call(
        functools.partial(forward_kernel, images=images, head_dim=head_dim, masked=masked, spill=spill),
        out_shape=(shapes[0], *(pltpu.HBM(part.shape, part.dtype) if spill else part for part in shapes[1:])),
        in_specs=[smem()] + [vmem()] * 8,
        out_specs=(vmem(), *(hbm() if spill else vmem() for _ in shapes[1:])),
        scratch_shapes=scratch,
        compiler_params=SPILL_PARAMS if spill else PARAMS,
        cost_estimate=busy(13),
        name="layer_forward",
    )(base, rows_in, perm, bias, vec, wqkv, wout, wup, wdown)


def run_ffn_back(base, g_rows, live, perm, vec, weights, kept, images, fetch):
    _, wout, wup, wdown = weights
    _, _, _, _, mix, res, n2, act, slope = kept
    width, hidden = wup.shape
    total = images * IROWS
    shapes = (
        shape_of((total, width), F32),
        shape_of((total, width), BF16),
        shape_of((hidden + width // 2, width), BF16),
        shape_of((hidden + width // 2, width), BF16),
        shape_of((SMALL_ROWS, width), F32),
    )
    scratch = []
    if fetch:
        scratch = [pltpu.VMEM(part.shape, part.dtype) for part in (mix, res, n2, act, slope)]
        scratch.append(pltpu.SemaphoreType.DMA((5,)))
    return pl.pallas_call(
        functools.partial(ffn_back_kernel, images=images),
        out_shape=shapes,
        in_specs=[smem(), vmem(), smem()] + [vmem()] * 5 + [hbm() if fetch else vmem()] * 5,
        out_specs=tuple(vmem() for _ in shapes),
        scratch_shapes=[
            pltpu.VMEM((total, width), BF16),
            pltpu.VMEM((total, hidden), BF16),
            pltpu.VMEM((total, width), BF16),
        ] + scratch,
        compiler_params=PARAMS,
        cost_estimate=busy(9),
        name="ffn_back",
    )(base, g_rows, live, perm, vec, wout, wup, wdown, mix, res, n2, act, slope)


def run_attn_back(base, perm, vec, weights, kept, dres, dmix, images, head_dim):
    wqkv = weights[0]
    xa, nrm, qkv, prob = kept[:4]
    width = wqkv.shape[0]
    total = images * IROWS
    shapes = (
        shape_of((images, SIDE * SIDE, width), F32),
        shape_of((images, SIDE * SIDE, width), BF16),
        shape_of((3 * width // 2, width), BF16),
        shape_of((3 * width // 2, width), BF16),
        shape_of((width // LANES, PADW, GROUP * PADW), F32),
        shape_of((SMALL_ROWS, width), F32),
    )
    return pl.pallas_call(
        functools.partial(attn_back_kernel, images=images, head_dim=head_dim),
        out_shape=shapes,
        in_specs=[smem()] + [vmem()] * 9,
        out_specs=tuple(vmem() for _ in shapes),
        scratch_shapes=[pltpu.VMEM((total, 3 * width), BF16)],
        compiler_params=PARAMS,
        cost_estimate=busy(13),
        name="attn_back",
    )(base, perm, vec, wqkv, xa, nrm, qkv, prob, dres, dmix)


def round_orders(bits):
    if bits == 4:
        return ((0, 1, 2, 3), (1, 0, 3, 2), (2, 3, 0, 1), (3, 2, 0, 1))
    axes = list(range(bits))
    return tuple(tuple(axes[turn:] + axes[:turn]) for turn in range(4))


def added(left, right):
    return (left.astype(F32) + right.astype(F32)).astype(BF16)


def first_ffn_kernel(bit_ref, keep_ref, recv_ref, *outs, turn):
    tail_ref = outs[4]
    for color in range(2):
        half = outs[color].shape[0]
        bit = bit_ref[turn + color]
        for side, place in ((0, bit), (2, 1 - bit)):
            rows = pl.ds(pl.multiple_of(color * 2 * half + place * half, half), half)
            outs[side + color][...] = added(keep_ref[rows, :], recv_ref[rows, :])
    tail = keep_ref.shape[0] - tail_ref.shape[0]
    tail_ref[...] = added(keep_ref[tail:, :], recv_ref[tail:, :])


def first_qkv_kernel(bit_ref, tail_ref, keep_ref, recv_ref, *outs, turn):
    half = outs[0].shape[0]
    head = added(keep_ref[:half, :], recv_ref[:half, :])
    low = bit_ref[turn + 2] == 0
    outs[0][...] = jnp.where(low, tail_ref[...], head)
    outs[2][...] = jnp.where(low, head, tail_ref[...])
    bit = bit_ref[turn + 3]
    for side, place in ((1, bit), (3, 1 - bit)):
        rows = pl.ds(pl.multiple_of(half + place * half, half), half)
        outs[side][...] = added(keep_ref[rows, :], recv_ref[rows, :])


def sum_kernel(bit_ref, *refs, turn):
    keep, recv, outs = refs[:4], refs[4:8], refs[8:]
    for color in range(4):
        half = keep[color].shape[0] // 2
        bit = bit_ref[turn + color]
        for side, start in ((0, bit * half), (4, (1 - bit) * half)):
            rows = pl.ds(pl.multiple_of(start, 8), half)
            outs[side + color][...] = added(keep[color][rows, :], recv[color][rows, :])


def last_kernel(bit_ref, *refs, turn):
    keep, recv, out_ref = refs[:4], refs[4:8], refs[8]
    at = 0
    for color in range(4):
        size = keep[color].shape[0]
        out_ref[at : at + size, :] = added(keep[color][...], recv[color][...])
        at += size


def split_small(value):
    high = value.astype(BF16)
    return high, (value - high.astype(F32)).astype(BF16)


def pick_kernel(section_ref, zero_ref, one_ref, small_zero_ref, small_one_ref, own_ref, send_ref, *, turn):
    first = section_ref[0] == 0
    size = zero_ref.shape[0]
    own_ref[:size, :] = jnp.where(first, zero_ref[...], one_ref[...])
    send_ref[:size, :] = jnp.where(first, one_ref[...], zero_ref[...])
    for dest, value in (
        (own_ref, jnp.where(first, small_zero_ref[...], small_one_ref[...])),
        (send_ref, jnp.where(first, small_one_ref[...], small_zero_ref[...])),
    ):
        high, low = split_small(value)
        dest[size : size + EXTRA, :] = high
        dest[size + EXTRA :, :] = low


def join_kernel(section_ref, own_ref, got_ref, *outs, turn):
    first = section_ref[0] == 0
    at = 0
    for color in range(4):
        size = outs[color].shape[1] - (EXTRA if color == 3 else 0)
        mine, other = own_ref[at : at + size, :], got_ref[at : at + size, :]
        outs[color][0, :size, :] = jnp.where(first, mine, other)
        outs[color][1, :size, :] = jnp.where(first, other, mine)
        at += size
    total = jnp.zeros((EXTRA, own_ref.shape[1]), F32)
    for ref in (own_ref, got_ref):
        total += ref[at : at + EXTRA, :].astype(F32) + ref[at + EXTRA :, :].astype(F32)
    high, low = split_small(total)
    outs[3][0, size:, :] = high
    outs[3][1, size:, :] = low


def small_total(own_ref, recv_ref):
    total = jnp.zeros((EXTRA, own_ref.shape[2]), F32)
    at = own_ref.shape[1] - EXTRA
    for ref in (own_ref, recv_ref):
        total += ref[0, at:, :].astype(F32) + ref[1, at:, :].astype(F32)
    return total


def merge_kernel(bit_ref, *refs, turn):
    own, recv, outs = refs[:4], refs[4:8], refs[8:]
    for color in range(4):
        size = own[color].shape[1] - (EXTRA if color == 3 else 0)
        bit = bit_ref[turn + color]
        outs[color][:, pl.ds(pl.multiple_of(bit * size, 8), size), :] = own[color][:, :size, :]
        outs[color][:, pl.ds(pl.multiple_of((1 - bit) * size, 8), size), :] = recv[color][:, :size, :]
    high, low = split_small(small_total(own[3], recv[3]))
    outs[3][0, 2 * size :, :] = high
    outs[3][1, 2 * size :, :] = low


def final_kernel(bit_ref, *refs, turn):
    own, recv = refs[:4], refs[4:8]
    down_ref, up_ref, out_ref, qkv_ref = refs[8:12]
    rows_refs, up_bias_ref, table_ref = refs[12:20], refs[20], refs[21]
    width = out_ref.shape[1]
    part = width // 2
    for half in range(2):
        rows = slice(half * part, (half + 1) * part)
        bit = bit_ref[turn + 0]
        span = own[0].shape[1]
        for side, source in ((bit, own[0]), (1 - bit, recv[0])):
            down_ref[pl.ds(pl.multiple_of(half * 2 * span + side * span, span), span), :] = source[half].astype(F32)
        bit = bit_ref[turn + 1]
        blocks = own[1].shape[1] // part
        for side, source in ((bit, own[1]), (1 - bit, recv[1])):
            for block in range(blocks):
                cols = pl.ds(pl.multiple_of((side * blocks + block) * width, width), width)
                up_ref[rows, cols] = source[half, block * part : (block + 1) * part, :].astype(F32)
        is_low = bit_ref[turn + 2] == 0
        mine, other = own[2][half].astype(F32), recv[2][half].astype(F32)
        out_ref[rows, :] = jnp.where(is_low, mine, other)
        qkv_ref[rows, :width] = jnp.where(is_low, other, mine)
        bit = bit_ref[turn + 3]
        size = own[3].shape[1] - EXTRA
        for side, source in ((bit, own[3]), (1 - bit, recv[3])):
            cols = pl.ds(pl.multiple_of((1 + side) * width, width), width)
            qkv_ref[rows, cols] = source[half, :size, :].astype(F32)
    total = small_total(own[3], recv[3])
    for number, ref in enumerate(rows_refs):
        ref[...] = total[number : number + 1, :]
    for block in range(up_bias_ref.shape[1] // width):
        up_bias_ref[:, block * width : (block + 1) * width] = total[8 + block : 9 + block, :]
    table_ref[...] = total[SMALL_ROWS:, : table_ref.shape[1]]


def small_call(kernel, bits, arrays, shapes, turn=0):
    return pl.pallas_call(
        functools.partial(kernel, turn=4 * turn),
        out_shape=tuple(shapes),
        in_specs=[smem()] + [vmem()] * len(arrays),
        out_specs=tuple(vmem() for _ in shapes),
        compiler_params=SMALL_PARAMS,
    )(bits, *arrays)


def exchange(value, bit, count):
    return lax.ppermute(value, "dp", [(one, one ^ (1 << bit)) for one in range(count)])


def start_rounds(keep_ffn, send_ffn, keep_qkv, send_qkv, place_bits):
    width = keep_ffn.shape[1]
    recv_ffn = swap(send_ffn)
    recv_qkv = swap(send_qkv)
    long = shape_of(((keep_ffn.shape[0] - width // 2) // 4, width), BF16)
    short = shape_of((width // 2, width), BF16)
    *ffn, tail = small_call(first_ffn_kernel, place_bits, (keep_ffn, recv_ffn), [long] * 4 + [short])
    rest = small_call(first_qkv_kernel, place_bits, (tail, keep_qkv, recv_qkv), [short] * 4)
    return (*ffn[:2], *rest[:2], *ffn[2:], *rest[2:])


def reduce_rounds(parts, orders, place_bits, count):
    width = parts[0].shape[1]
    rounds = len(orders[0])
    for turn in range(rounds):
        mine, gone = parts[:4], parts[4:]
        recv = [exchange(part, order[turn], count) for part, order in zip(gone, orders)]
        if turn + 1 < rounds:
            halves = [shape_of((part.shape[0] // 2, width), BF16) for part in mine]
            parts = small_call(sum_kernel, place_bits, list(mine) + recv, halves * 2, turn + 1)
        else:
            total = shape_of((sum(part.shape[0] for part in mine), width), BF16)
            parts = small_call(last_kernel, place_bits, list(mine) + recv, [total])
    return parts[0]


def gather_layer(shard_zero, shard_one, small_zero, small_one, where, sizes, hidden, entries, heads, orders, place_bits, count):
    rows, width = shard_zero.shape
    both_shape = [shape_of((rows + 2 * EXTRA, width), BF16)] * 2
    own, send = small_call(pick_kernel, where, (shard_zero, shard_one, small_zero, small_one), both_shape)
    got = swap(send)
    extras = (0, 0, 0, EXTRA)
    shapes = [shape_of((2, size + extra, width), BF16) for size, extra in zip(sizes, extras)]
    parts = small_call(join_kernel, where, (own, got), shapes)
    rounds = len(orders[0])
    for turn in reversed(range(rounds)):
        recv = []
        for part, order in zip(parts, orders):
            recv.append(exchange(part, order[turn], count))
        if turn:
            shapes = [
                shape_of((2, 2 * part.shape[1] - extra, width), BF16) for part, extra in zip(parts, extras)
            ]
            parts = small_call(merge_kernel, place_bits, list(parts) + recv, shapes, turn)
    shapes = [shape_of((hidden, width), F32), shape_of((width, hidden), F32), shape_of((width, width), F32),
              shape_of((width, 3 * width), F32)]
    shapes += [shape_of((1, width), F32)] * 8 + [shape_of((1, hidden), F32), shape_of((heads, entries), F32)]
    return small_call(final_kernel, place_bits, list(parts) + recv, shapes)


def swap(value):
    return lax.ppermute(value, "section", [(0, 1), (1, 0)])


def weights_kernel(section_ref, *refs):
    own, got, zero, one, sem = refs[:4], refs[4:8], refs[8:12], refs[12:16], refs[16]

    def copy_all(first, second):
        copies = [
            pltpu.make_async_copy(source, dest, sem.at[number])
            for number, (source, dest) in enumerate(zip((*first, *second), (*zero, *one)))
        ]
        for copy in copies:
            copy.start()
        for copy in copies:
            copy.wait()

    @pl.when(section_ref[0] == 0)
    def _():
        copy_all(own, got)

    @pl.when(section_ref[0] != 0)
    def _():
        copy_all(got, own)


def both_weights(weights, where):
    got = [swap(weight) for weight in weights]
    shapes = [shape_of(weight.shape, weight.dtype) for weight in weights] * 2
    picked = pl.pallas_call(
        weights_kernel,
        out_shape=tuple(shapes),
        in_specs=[smem()] + [pl.BlockSpec(memory_space=pl.ANY)] * 8,
        out_specs=tuple(vmem() for _ in shapes),
        scratch_shapes=[pltpu.SemaphoreType.DMA((8,))],
        compiler_params=SMALL_PARAMS,
        name="pick_weights",
    )(where, *weights, *got)
    return picked[:4], picked[4:]


def both(value, section):
    other = swap(value)
    first = jnp.where(section == 0, value, other)
    second = jnp.where(section == 0, other, value)
    return first, second


def body(
    images,
    cotangent,
    image_count,
    norm1_gain,
    norm1_bias,
    qkv_weight,
    query_bias,
    value_bias,
    bias_table,
    out_weight,
    out_bias,
    norm2_gain,
    norm2_bias,
    up_weight,
    up_bias,
    down_weight,
    down_bias,
):
    section = lax.axis_index("section")
    slots = images.shape[0]
    mine = slots // 2
    width = images.shape[-1]
    heads = bias_table.shape[-1]
    head_dim = width // heads
    vectors = jnp.concatenate(
        [norm1_gain, norm1_bias, query_bias, value_bias, out_bias, norm2_gain, norm2_bias, down_bias,
         up_bias.reshape(-1, width)], axis=0)
    layer_vec = both(vectors, section)
    layer_table = both(bias_table[0], section)
    where = section.astype(jnp.int32).reshape(1)
    layer_w = both_weights([weight[0] for weight in (qkv_weight, out_weight, up_weight, down_weight)], where)
    perms = [jnp.asarray(window_onehot(shift), BF16) for shift in (0, SHIFT)]
    onehot = pair_onehot()
    biases = bias_tiles(jnp.stack(layer_table), onehot)
    base_mine = jnp.stack([section * mine, section]).astype(jnp.int32)
    base_zero = jnp.stack([section * 0, section]).astype(jnp.int32)
    live = (section * mine + jnp.arange(mine) < image_count[0]).astype(F32)
    ones = jnp.ones((mine,), F32)
    count = lax.axis_size("dp")
    bits = count.bit_length() - 1
    chip = lax.axis_index("dp")
    orders = round_orders(bits)
    turns = np.array([[order[turn] for order in orders] for turn in range(bits)]).reshape(-1)
    place_bits = (chip >> turns.astype(np.int32)) & 1

    out_zero, *kept_zero = run_forward(base_mine, images, perms[0], biases[0], layer_vec[0], layer_w[0], mine, head_dim, False)
    out_one, *kept_one = run_forward(base_zero, out_zero, perms[1], biases[1], layer_vec[1], layer_w[1], mine, head_dim, True)

    def backward(layer, base, g_rows, alive, kept):
        dres, dmix, keep_ffn, send_ffn, small_ffn = run_ffn_back(
            base, g_rows, alive, perms[layer], layer_vec[layer], layer_w[layer], kept, mine, layer == 0)
        igrad, igrad_b, keep_qkv, send_qkv, tiles, small_attn = run_attn_back(
            base, perms[layer], layer_vec[layer], layer_w[layer], kept, dres, dmix, mine, head_dim)
        parts = start_rounds(keep_ffn, send_ffn, keep_qkv, send_qkv, place_bits)
        shard = reduce_rounds(parts, orders, place_bits, count)
        return igrad, igrad_b, shard, (tiles, small_ffn + small_attn), parts

    igrad_one, back_rows, shard_one, rest_one, parts = backward(1, base_mine, cotangent, live, kept_one)
    halves = [part.shape[0] for part in parts[:4]]
    igrad_zero, _, shard_zero, rest_zero, parts = backward(0, base_zero, back_rows, ones, kept_zero)

    def finish_small(rest):
        (tiles, vecs), _ = lax.optimization_barrier((rest, parts[2]))
        table = table_grad(tiles, heads, onehot)
        return jnp.concatenate([vecs, jnp.pad(table, ((0, 0), (0, width - table.shape[1])))])

    small_zero, small_one = finish_small(rest_zero), finish_small(rest_one)

    hidden = up_bias.shape[1]
    sizes = [half >> (bits - 1) for half in halves]
    g_down, g_up, g_out, g_qkv, *vecs, g_up_b, g_table = gather_layer(
        shard_zero, shard_one, small_zero, small_one, where, sizes, hidden, bias_table.shape[1], heads, orders,
        place_bits, count)

    def place(first, second):
        got = swap(jnp.where(section == 0, second, first))
        upper = jnp.concatenate([first, got], axis=0)
        lower = jnp.concatenate([got, second], axis=0)
        return jnp.where(section == 0, upper, lower)

    segment_out = place(out_zero, out_one)
    input_grad = place(igrad_zero, igrad_one)
    g_gain_one, g_bias_one, g_query, g_value, g_out_b, g_gain_two, g_bias_two, g_down_b = vecs
    return (
        segment_out[None], input_grad[None], g_gain_one, g_bias_one, g_qkv[None], g_query, g_value, g_table.T[None],
        g_out[None], g_out_b, g_gain_two, g_bias_two, g_up[None], g_up_b, g_down[None], g_down_b,
    )


def solution(mesh):
    row = P("section", None)
    mat = P("section", None, None)

    return jax.shard_map(
        body,
        mesh=mesh,
        in_specs=(
            P("dp", None, None), P("dp", None, None), P("dp"),
            row, row, mat, row, row, mat, mat, row, row, row, mat, row, mat, row,
        ),
        out_specs=(
            P("section", "dp", None, None), P("section", "dp", None, None),
            row, row, mat, row, row, mat, mat, row, row, row, mat, row, mat, row,
        ),
        check_vma=False,
    )
```
